256 devices in a mesh: sector: 16 (over z, x_lo), row: 16 (over x_hi, y, core).
Axes of the slice: x: 4 (x_hi: 2, x_lo: 2; x = x_hi * 2 + x_lo), y: 4, z: 8, core: 2. Of those that a mesh axis runs over, the one named last changes fastest.
Arguments:
- cosine_load: float32 [16384, 128], P('row'), may hold values from -6 to 6
- sine_load: float32 [16384, 128], P('row'), may hold values from -6 to 6
- base_stiffness: float32 [16384], P('row'), may hold values from 1 to 3
- coupling_ratio: float32 [16384], P('row'), may hold values from 0.35 to 0.42
- mistuning: float32 [4, 16384], P(None, 'row'), may hold values from -0.1 to 0.1
- sector_class: int32 [16], P('sector'), may hold values from 0 to 3
- engine_order: int32 [1], replicated, may hold values from 1 to 7
- block_values: bfloat16 [16, 64, 16, 256, 256], P('sector', 'row'), may hold values from -0.03125 to 0.03125
- block_columns: int32 [64, 16], P('row'), may hold values from 0 to 63, all different within a row
Outputs:
- solution: float32 [16, 16384, 128], P('sector', 'row')
The draws below stay inside these ranges and needn't reach their ends.
Inputs may be any that keep to these rules, and one draw needn't show every extreme that they name: `block_columns`: each block row lists 16 distinct block columns; every block column is listed by some block row.
All inputs are finite; a program needn't handle non-finite values.
Results may differ from the reference program's by a relative error of at most 0.0015.
Values may be sent and summed in bfloat16 or wider, within the bound.
No kernel may reach another device: no remote copies, remote signals or barrier semaphores. Data moves between devices by JAX's collectives and lax.ppermute only.
A program may use at most 64 MiB of HBM per device.

```python
import math
import jax
import jax.numpy as jnp
from jax import lax

DOF = 16384
BLK = 256
K = 16
NRHS = 128
ITERS = 4
LEVELS = 3
CLASSES = 4
SECTORS = 16
NBLK = 64


def plant(drawn, rng, least, top_value):
    shape = drawn.shape
    index_at = [jax.random.randint(jax.random.fold_in(rng, axis), (), 0, shape[axis]) for axis in range(len(shape))]
    drawn = drawn.at[tuple(index_at)].set(least)
    longest = shape.index(max(shape))
    index_at[longest] = (index_at[longest] + 1) % shape[longest]
    return drawn.at[tuple(index_at)].set(top_value)


def level_of(own_key, shape, cuts, least, top_value):
    factor_of, own = 1.0, jax.random.fold_in(own_key, 6)
    for dim, shards_of in cuts:
        steps = jnp.exp(jax.random.uniform(jax.random.fold_in(own, dim), (shards_of,), jnp.float32, least / len(cuts), top_value / len(cuts)))
        factor_of = factor_of * jnp.repeat(steps, shape[dim] // shards_of).reshape([-1 if axis == dim else 1 for axis in range(len(shape))])
    return factor_of


def picks_of(own_key, rows, count, top, lift):
    ranking = jax.random.permutation(jax.random.fold_in(own_key, 1), count)
    favour = ranking
    for power in range(3):
        favour = favour * favour // count
    favour = favour * lift // count
    tickets = jax.random.randint(jax.random.fold_in(own_key, 2), (rows, count), 0, 4096) + favour
    sure = jax.random.permutation(jax.random.fold_in(own_key, 3), rows)[jnp.arange(count) % rows]
    tickets = jnp.where(jnp.arange(rows)[:, None] == sure[None, :], 1 << 14, tickets)
    priority = tickets * count + jnp.arange(count)
    return lax.top_k(priority.astype(jnp.int32), top)[1].astype(jnp.int32)


def normal_values(own_key, extent, width, most, split=(), kind=jnp.bfloat16):
    loudness = level_of(own_key, extent, split, -0.22, 0.18) if split else 1.0
    array = jax.random.normal(own_key, extent, jnp.float32) * width * loudness
    return jnp.minimum(jnp.maximum(array, -most), most).astype(kind)


def setup_inputs(seed: int = 0) -> dict:
    key_list = jax.random.split(jax.random.key(seed), 10)
    return {
        "cosine_load": normal_values(key_list[0], (DOF, NRHS), 1.0, 6.0, ((0, 16),), jnp.float32),
        "sine_load": normal_values(key_list[1], (DOF, NRHS), 1.0, 6.0, ((0, 16),), jnp.float32),
        "base_stiffness": jnp.clip(jnp.exp(math.log(3.0) - 1.0986123 * jax.random.uniform(key_list[2], (DOF,), jnp.float32) ** level_of(key_list[2], (DOF,), ((0, 16),), -0.2, 0.2)), 1.0, 3.0),
        "coupling_ratio": jnp.clip(0.35 + 0.06999999 * jax.random.uniform(key_list[3], (DOF,), jnp.float32) ** level_of(key_list[3], (DOF,), ((0, 16),), -0.2, 0.2), 0.35, 0.42),
        "mistuning": jnp.clip(jax.random.uniform(key_list[4], (CLASSES, DOF), jnp.float32, -0.1, 0.1) * level_of(key_list[4], (CLASSES, DOF), ((1, 16),), -0.4, 0.0), -0.1, 0.1),
        "sector_class": plant(jax.random.randint(key_list[5], (SECTORS,), 0, CLASSES), jax.random.fold_in(key_list[5], 1), 0, CLASSES - 1).astype(jnp.int32),
        "engine_order": jax.random.randint(key_list[6], (1,), 1, SECTORS // 2).astype(jnp.int32),
        "block_values": normal_values(key_list[7], (SECTORS, NBLK, K, BLK, BLK), (8 * K * BLK) ** -0.5, 0.03125, ((0, 16), (1, 16))),
        "block_columns": picks_of(key_list[8], NBLK, NBLK, K, 0),
    }


def reduce_coefficients(sub_diag, main_diag, super_diag):
    factors = []
    for exponent in range(LEVELS):
        stride = 2 ** exponent
        lower_factor = -sub_diag / jnp.roll(main_diag, stride, 0)
        upper_factor = -super_diag / jnp.roll(main_diag, -stride, 0)
        factors.append((lower_factor, upper_factor))
        sub_diag, main_diag, super_diag = (
            lower_factor * jnp.roll(sub_diag, stride, 0),
            main_diag + lower_factor * jnp.roll(super_diag, stride, 0) + upper_factor * jnp.roll(sub_diag, -stride, 0),
            upper_factor * jnp.roll(super_diag, -stride, 0),
        )
    return factors, main_diag


def apply_reduction(factors, reduced, right_side):
    for exponent in range(LEVELS):
        stride = 2 ** exponent
        lower_factor, upper_factor = factors[exponent]
        right_side = right_side + lower_factor[..., None] * jnp.roll(right_side, stride, 0) + upper_factor[..., None] * jnp.roll(right_side, -stride, 0)
    return right_side / reduced[..., None]


def reference(cosine_load, sine_load, base_stiffness, coupling_ratio, mistuning, sector_class, engine_order, block_values, block_columns):
    sector_ids = jnp.arange(SECTORS, dtype=jnp.int32)
    sector_turns = ((engine_order[0] * sector_ids) % SECTORS).astype(jnp.float32)
    sector_angle = sector_turns * (2.0 * math.pi / SECTORS)
    forcing = jnp.cos(sector_angle)[:, None, None] * cosine_load[None] + jnp.sin(sector_angle)[:, None, None] * sine_load[None]
    diagonal = base_stiffness[None] * (1.0 + mistuning[sector_class])
    coupling = coupling_ratio * base_stiffness
    cycle_coupling = jnp.broadcast_to(-coupling[None], diagonal.shape)
    factors, reduced = reduce_coefficients(cycle_coupling, diagonal, cycle_coupling)

    def sector_product(operands):
        values, rounded_sector = operands
        column_tiles = rounded_sector.reshape(NBLK, BLK, NRHS)[block_columns]
        product = jnp.einsum("rkij,rkjc->ric", values.astype(jnp.float32), column_tiles.astype(jnp.float32), precision=lax.Precision.HIGHEST)
        return product.reshape(DOF, NRHS)

    def apply_operator(current):
        rounded = current.astype(jnp.bfloat16)
        product = lax.map(sector_product, (block_values, rounded))
        return diagonal[..., None] * current - coupling[None, :, None] * (jnp.roll(current, 1, 0) + jnp.roll(current, -1, 0)) + product

    solution = jnp.zeros((SECTORS, DOF, NRHS), jnp.float32)
    for iteration in range(ITERS):
        if iteration == 0:
            residual = forcing
        else:
            residual = forcing - apply_operator(solution)
        solution = solution + apply_reduction(factors, reduced, residual)
    return solution
```

```python
import math

import jax
import jax.numpy as jnp
from jax import lax
from jax.experimental import pallas as pl
from jax.experimental.pallas import tpu as pltpu
from jax.sharding import PartitionSpec as P

ITERS = 4
LEVELS = 3
ROW_PARTS = (2, 4, 2)


def row_peers(shift_x, shift_y, shift_core):
    pairs = []
    for x in range(ROW_PARTS[0]):
        for y in range(ROW_PARTS[1]):
            for core in range(ROW_PARTS[2]):
                source = (
                    ((x + shift_x) % ROW_PARTS[0] * ROW_PARTS[1] + (y + shift_y) % ROW_PARTS[1])
                    * ROW_PARTS[2]
                    + (core + shift_core) % ROW_PARTS[2]
                )
                target = (x * ROW_PARTS[1] + y) * ROW_PARTS[2] + core
                pairs.append((source, target))
    return pairs


def gather_pieces(own):
    same_core = [own]
    for shift_x in range(ROW_PARTS[0]):
        for shift_y in range(ROW_PARTS[1]):
            if shift_x or shift_y:
                same_core.append(lax.ppermute(own, "row", row_peers(shift_x, shift_y, 0)))
    other_core = [lax.ppermute(piece, "row", row_peers(0, 0, 1)) for piece in same_core]
    return same_core + other_core


def relative_columns(block_columns, blocks_per_device):
    row_id = lax.axis_index("row")
    owner = block_columns // blocks_per_device
    cores, ys = ROW_PARTS[2], ROW_PARTS[1]
    core = (owner - row_id) % cores
    shift_y = (owner // cores - row_id // cores) % ys
    shift_x = (owner // (cores * ys) - row_id // (cores * ys)) % ROW_PARTS[0]
    piece = (core * ROW_PARTS[0] + shift_x) * ys + shift_y
    return piece * blocks_per_device + block_columns % blocks_per_device


def product_kernel(columns, values, *refs):
    pieces, out, tiles = refs[:-2], refs[-2], refs[-1]
    rows, count, order, _ = values.shape
    per_piece = pieces[0].shape[0] // order
    for index, piece in enumerate(pieces):
        for part in range(per_piece):
            tiles[index * per_piece + part] = piece[part * order : (part + 1) * order, :]

    def one_row(row, carry):
        total = None
        for k in range(count):
            term = jnp.dot(
                values[row, k],
                tiles[columns[row * count + k]],
                preferred_element_type=jnp.float32,
            )
            total = term if total is None else total + term
        out[pl.ds(pl.multiple_of(row * order, order), order), :] = total
        return carry

    lax.fori_loop(0, rows, one_row, 0)


def block_product(block_values, columns, pieces):
    rows, count, order, _ = block_values.shape
    load_cases = pieces[0].shape[1]
    vmem = pl.BlockSpec(memory_space=pltpu.VMEM)
    return pl.pallas_call(
        product_kernel,
        out_shape=jax.ShapeDtypeStruct((rows * order, load_cases), jnp.float32),
        in_specs=[pl.BlockSpec(memory_space=pltpu.SMEM), vmem] + [vmem] * len(pieces),
        out_specs=vmem,
        scratch_shapes=[
            pltpu.VMEM(
                (len(pieces) * pieces[0].shape[0] // order, order, load_cases), jnp.bfloat16
            )
        ],
        compiler_params=pltpu.CompilerParams(vmem_limit_bytes=32 * 1024 * 1024),
        cost_estimate=pl.CostEstimate(
            flops=2 * rows * count * order * order * load_cases,
            bytes_accessed=2 * rows * count * order * order,
            transcendentals=0,
        ),
    )(columns, block_values, *pieces)


def reduce_coefficients(sub_diag, main_diag, super_diag):
    factors = []
    for exponent in range(LEVELS):
        stride = 2**exponent
        lower_factor = -sub_diag / jnp.roll(main_diag, stride, 0)
        upper_factor = -super_diag / jnp.roll(main_diag, -stride, 0)
        factors.append((lower_factor, upper_factor))
        sub_diag, main_diag, super_diag = (
            lower_factor * jnp.roll(sub_diag, stride, 0),
            main_diag
            + lower_factor * jnp.roll(super_diag, stride, 0)
            + upper_factor * jnp.roll(sub_diag, -stride, 0),
            upper_factor * jnp.roll(super_diag, -stride, 0),
        )
    return factors, main_diag


def apply_reduction(factors, reduced, right_side):
    for exponent in range(LEVELS):
        stride = 2**exponent
        lower_factor, upper_factor = factors[exponent]
        right_side = (
            right_side
            + lower_factor * jnp.roll(right_side, stride, 0)
            + upper_factor * jnp.roll(right_side, -stride, 0)
        )
    return right_side / reduced


def shards(
    cosine_load,
    sine_load,
    base_stiffness,
    coupling_ratio,
    mistuning,
    sector_class,
    engine_order,
    block_values,
    block_columns,
):
    sectors = lax.axis_size("sector")
    sector_id = lax.axis_index("sector")
    local_rows, load_cases = cosine_load.shape
    slice_rows = local_rows // sectors
    order = block_values.shape[-1]

    def swap(cells):
        return lax.all_to_all(cells, "sector", 0, 0, tiled=True)

    def own_slice(cells, axis):
        return lax.dynamic_slice_in_dim(cells, sector_id * slice_rows, slice_rows, axis)

    all_classes = swap(jnp.broadcast_to(sector_class[:, None], (sectors, 1)))
    turns = (engine_order[0] * jnp.arange(sectors, dtype=jnp.int32)) % sectors
    angle = turns.astype(jnp.float32) * (2.0 * math.pi / sectors)
    cosine, sine = jnp.cos(angle)[:, None], jnp.sin(angle)[:, None]

    classes = mistuning.shape[0]
    picked = sum(
        jnp.where(all_classes == index, mistuning[index][None], 0.0) for index in range(classes)
    )
    diagonal = base_stiffness[None] * (1.0 + picked)
    coupling = coupling_ratio * base_stiffness
    cycle = jnp.broadcast_to(-coupling[None], diagonal.shape)
    factors, reduced = reduce_coefficients(cycle, diagonal, cycle)
    cosine_gain = apply_reduction(factors, reduced, jnp.broadcast_to(cosine, diagonal.shape))
    sine_gain = apply_reduction(factors, reduced, jnp.broadcast_to(sine, diagonal.shape))

    own_cosine = lax.dynamic_index_in_dim(cosine_gain, sector_id, 0, keepdims=False)
    own_sine = lax.dynamic_index_in_dim(sine_gain, sector_id, 0, keepdims=False)
    rounded = (own_cosine[:, None] * cosine_load + own_sine[:, None] * sine_load).astype(
        jnp.bfloat16
    )

    cosine_slice, sine_slice = own_slice(cosine_load, 0)[None], own_slice(sine_load, 0)[None]

    def spread(cells):
        return own_slice(cells, 1)[:, :, None]

    slice_factors = [(spread(lower), spread(upper)) for lower, upper in factors]
    slice_reduced, slice_diagonal = spread(reduced), spread(diagonal)
    slice_coupling = own_slice(coupling, 0)[None, :, None]
    forcing = cosine[:, :, None] * cosine_slice + sine[:, :, None] * sine_slice
    current = spread(cosine_gain) * cosine_slice + spread(sine_gain) * sine_slice

    columns = relative_columns(block_columns, block_values.shape[1]).reshape(-1)
    for iteration in range(1, ITERS):
        product = block_product(block_values[0], columns, gather_pieces(rounded))
        product = swap(product.reshape(sectors, slice_rows, load_cases))
        neighbours = jnp.roll(current, 1, 0) + jnp.roll(current, -1, 0)
        residual = forcing - (slice_diagonal * current - slice_coupling * neighbours + product)
        current = current + apply_reduction(slice_factors, slice_reduced, residual)
        if iteration < ITERS - 1:
            rounded = swap(current.astype(jnp.bfloat16)).reshape(local_rows, load_cases)
    return swap(current).reshape(1, local_rows, load_cases)


def solution(mesh):
    return jax.shard_map(
        shards,
        mesh=mesh,
        in_specs=(
            P("row", None),
            P("row", None),
            P("row"),
            P("row"),
            P(None, "row"),
            P("sector"),
            P(),
            P("sector", "row", None, None, None),
            P("row", None),
        ),
        out_specs=P("sector", "row", None),
        check_vma=False,
    )
```

```python
import math

import jax
import jax.numpy as jnp
from jax import lax
from jax.experimental import pallas as pl
from jax.experimental.pallas import tpu as pltpu
from jax.sharding import PartitionSpec as P

ITERS = 4
LEVELS = 3
ROW_PARTS = (2, 4, 2)


def row_peers(shift_x, shift_y, shift_core):
    pairs = []
    for x in range(ROW_PARTS[0]):
        for y in range(ROW_PARTS[1]):
            for core in range(ROW_PARTS[2]):
                source = (
                    ((x + shift_x) % ROW_PARTS[0] * ROW_PARTS[1] + (y + shift_y) % ROW_PARTS[1])
                    * ROW_PARTS[2]
                    + (core + shift_core) % ROW_PARTS[2]
                )
                target = (x * ROW_PARTS[1] + y) * ROW_PARTS[2] + core
                pairs.append((source, target))
    return pairs


SHIFTS = ((0, 0), (1, 0), (0, 2), (0, 1), (0, 3), (1, 1), (1, 3), (1, 2))


def gather_pieces(own):
    def fetch(block, *shift):
        return lax.ppermute(block, "row", row_peers(*shift))

    across = fetch(own, 1, 0, 0)
    opposite, above, below = fetch(own, 0, 2, 0), fetch(own, 0, 1, 0), fetch(own, 0, 3, 0)
    relayed = [fetch(across, 0, 1, 0), fetch(across, 0, 3, 0), fetch(opposite, 1, 0, 0)]
    same_core = [own, across, *lax.optimization_barrier([opposite, above, below, *relayed])]
    same_core = jnp.concatenate(same_core, axis=0)
    return [same_core, fetch(same_core, 0, 0, 1)]


def relative_columns(block_columns, blocks_per_device):
    row_id = lax.axis_index("row")
    owner = block_columns // blocks_per_device
    xs, ys, cores = ROW_PARTS
    core = (owner - row_id) % cores
    shift_y = (owner // cores - row_id // cores) % ys
    shift_x = (owner // (cores * ys) - row_id // (cores * ys)) % xs
    piece = sum(
        jnp.where((shift_x == x) & (shift_y == y), index, 0) for index, (x, y) in enumerate(SHIFTS)
    )
    return (core * len(SHIFTS) + piece) * blocks_per_device + block_columns % blocks_per_device


def product_kernel(columns, values, *refs):
    *pieces, out, tiles, held, arrived, collected = refs
    rows, count, order, _ = values.shape

    def fetch(row):
        return pltpu.make_async_copy(values.at[row], held.at[row], arrived.at[row])

    places, place = [], 0
    for index, piece in enumerate(pieces):
        span = piece.shape[0]
        places.append(
            pltpu.make_async_copy(piece, tiles.at[pl.ds(place, span)], collected.at[index])
        )
        place += span
    fetch(0).start()
    for copy in places:
        copy.start()
    for row in range(1, rows):
        fetch(row).start()
    for copy in places:
        copy.wait()

    def one_row(row, carry):
        fetch(row).wait()
        total = None
        for k in range(count):
            term = jnp.dot(
                held[row, k],
                tiles[columns[row * count + k]],
                preferred_element_type=jnp.float32,
            )
            total = term if total is None else total + term
        out[pl.ds(pl.multiple_of(row * order, order), order), :] = total
        return carry

    lax.fori_loop(0, rows, one_row, 0)


def block_product(block_values, columns, pieces):
    rows, count, order, _ = block_values.shape
    load_cases = pieces[0].shape[1]
    pieces = [piece.reshape(-1, order, load_cases) for piece in pieces]
    tiles = sum(piece.shape[0] for piece in pieces)
    return pl.pallas_call(
        product_kernel,
        out_shape=jax.ShapeDtypeStruct((rows * order, load_cases), jnp.float32),
        in_specs=[pl.BlockSpec(memory_space=pltpu.SMEM)]
        + [pl.BlockSpec(memory_space=pl.ANY)] * (1 + len(pieces)),
        out_specs=pl.BlockSpec(memory_space=pltpu.VMEM),
        scratch_shapes=[
            pltpu.VMEM((tiles, order, load_cases), jnp.bfloat16),
            pltpu.VMEM((rows, count, order, order), jnp.bfloat16),
            pltpu.SemaphoreType.DMA((rows,)),
            pltpu.SemaphoreType.DMA((len(pieces),)),
        ],
        compiler_params=pltpu.CompilerParams(vmem_limit_bytes=48 * 1024 * 1024),
        cost_estimate=pl.CostEstimate(
            flops=2 * rows * count * order * order * load_cases,
            bytes_accessed=2 * rows * count * order * order,
            transcendentals=0,
        ),
    )(columns, block_values, *pieces)


def reduce_coefficients(sub_diag, main_diag, super_diag):
    factors = []
    for exponent in range(LEVELS):
        stride = 2**exponent
        lower_factor = -sub_diag / jnp.roll(main_diag, stride, 0)
        upper_factor = -super_diag / jnp.roll(main_diag, -stride, 0)
        factors.append((lower_factor, upper_factor))
        sub_diag, main_diag, super_diag = (
            lower_factor * jnp.roll(sub_diag, stride, 0),
            main_diag
            + lower_factor * jnp.roll(super_diag, stride, 0)
            + upper_factor * jnp.roll(sub_diag, -stride, 0),
            upper_factor * jnp.roll(super_diag, -stride, 0),
        )
    return factors, main_diag


def apply_reduction(factors, reduced, right_side):
    for exponent in range(LEVELS):
        stride = 2**exponent
        lower_factor, upper_factor = factors[exponent]
        right_side = (
            right_side
            + lower_factor * jnp.roll(right_side, stride, 0)
            + upper_factor * jnp.roll(right_side, -stride, 0)
        )
    return right_side / reduced


def shards(
    cosine_load,
    sine_load,
    base_stiffness,
    coupling_ratio,
    mistuning,
    sector_class,
    engine_order,
    block_values,
    block_columns,
):
    sectors = lax.axis_size("sector")
    sector_id = lax.axis_index("sector")
    local_rows, load_cases = cosine_load.shape
    slice_rows = local_rows // sectors
    order = block_values.shape[-1]

    def swap(cells):
        return lax.all_to_all(cells, "sector", 0, 0, tiled=True)

    def own_slice(cells, axis):
        return lax.dynamic_slice_in_dim(cells, sector_id * slice_rows, slice_rows, axis)

    all_classes = swap(jnp.broadcast_to(sector_class[:, None], (sectors, 1)))
    turns = (engine_order[0] * jnp.arange(sectors, dtype=jnp.int32)) % sectors
    angle = turns.astype(jnp.float32) * (2.0 * math.pi / sectors)
    cosine, sine = jnp.cos(angle)[:, None], jnp.sin(angle)[:, None]

    classes = mistuning.shape[0]
    picked = sum(
        jnp.where(all_classes == index, mistuning[index][None], 0.0) for index in range(classes)
    )
    diagonal = base_stiffness[None] * (1.0 + picked)
    coupling = coupling_ratio * base_stiffness
    cycle = jnp.broadcast_to(-coupling[None], diagonal.shape)
    factors, reduced = reduce_coefficients(cycle, diagonal, cycle)
    cosine_gain = apply_reduction(factors, reduced, jnp.broadcast_to(cosine, diagonal.shape))
    sine_gain = apply_reduction(factors, reduced, jnp.broadcast_to(sine, diagonal.shape))

    own_cosine = lax.dynamic_index_in_dim(cosine_gain, sector_id, 0, keepdims=False)
    own_sine = lax.dynamic_index_in_dim(sine_gain, sector_id, 0, keepdims=False)
    rounded = (own_cosine[:, None] * cosine_load + own_sine[:, None] * sine_load).astype(
        jnp.bfloat16
    )

    cosine_slice, sine_slice = own_slice(cosine_load, 0)[None], own_slice(sine_load, 0)[None]

    def spread(cells):
        return own_slice(cells, 1)[:, :, None]

    slice_factors = [(spread(lower), spread(upper)) for lower, upper in factors]
    slice_reduced, slice_diagonal = spread(reduced), spread(diagonal)
    slice_coupling = own_slice(coupling, 0)[None, :, None]
    forcing = cosine[:, :, None] * cosine_slice + sine[:, :, None] * sine_slice
    current = spread(cosine_gain) * cosine_slice + spread(sine_gain) * sine_slice

    columns = relative_columns(block_columns, block_values.shape[1]).reshape(-1)
    for iteration in range(1, ITERS):
        last = iteration == ITERS - 1
        product = block_product(block_values[0], columns, gather_pieces(rounded))
        if last:
            change = (product - earlier_product).astype(jnp.bfloat16)
            change = swap(change.reshape(sectors, slice_rows, load_cases))
            slice_product = slice_product + change.astype(jnp.float32)
        else:
            earlier_product = product
            slice_product = swap(product.reshape(sectors, slice_rows, load_cases))
        neighbours = jnp.roll(current, 1, 0) + jnp.roll(current, -1, 0)
        residual = forcing - (
            slice_diagonal * current - slice_coupling * neighbours + slice_product
        )
        sent = current.astype(jnp.bfloat16).astype(jnp.float32)
        current = current + apply_reduction(slice_factors, slice_reduced, residual)
        if not last:
            rounded = swap(current.astype(jnp.bfloat16)).reshape(local_rows, load_cases)
    difference = swap((current - sent).astype(jnp.bfloat16)).reshape(local_rows, load_cases)
    return (rounded.astype(jnp.float32) + difference.astype(jnp.float32))[None]


def solution(mesh):
    return jax.shard_map(
        shards,
        mesh=mesh,
        in_specs=(
            P("row", None),
            P("row", None),
            P("row"),
            P("row"),
            P(None, "row"),
            P("sector"),
            P(),
            P("sector", "row", None, None, None),
            P("row", None),
        ),
        out_specs=P("sector", "row", None),
        check_vma=False,
    )
```

```python
import math

import jax
import jax.numpy as jnp
from jax import lax
from jax.experimental import pallas as pl
from jax.experimental.pallas import tpu as pltpu
from jax.sharding import PartitionSpec as P

ITERS = 4
LEVELS = 3
ROW_PARTS = (2, 4, 2)


def row_peers(shift_x, shift_y, shift_core):
    pairs = []
    for x in range(ROW_PARTS[0]):
        for y in range(ROW_PARTS[1]):
            for core in range(ROW_PARTS[2]):
                source = (
                    ((x + shift_x) % ROW_PARTS[0] * ROW_PARTS[1] + (y + shift_y) % ROW_PARTS[1])
                    * ROW_PARTS[2]
                    + (core + shift_core) % ROW_PARTS[2]
                )
                target = (x * ROW_PARTS[1] + y) * ROW_PARTS[2] + core
                pairs.append((source, target))
    return pairs


SHIFTS = ((0, 0), (1, 0), (0, 2), (0, 1), (0, 3), (1, 1), (1, 3), (1, 2))


def gather_pieces(own):
    def fetch(block, *shift):
        return lax.ppermute(block, "row", row_peers(*shift))

    across = fetch(own, 1, 0, 0)
    opposite, above, below = fetch(own, 0, 2, 0), fetch(own, 0, 1, 0), fetch(own, 0, 3, 0)
    relayed = [fetch(across, 0, 1, 0), fetch(across, 0, 3, 0), fetch(opposite, 1, 0, 0)]
    direct = [own, across, opposite, above, below]
    order = direct + relayed
    swapped = [
        fetch(jnp.concatenate(part, axis=0), 0, 0, 1) for part in (order[:4], order[4:])
    ]
    return jnp.concatenate(direct + relayed + swapped, axis=0)


def relative_columns(block_columns, blocks_per_device):
    row_id = lax.axis_index("row")
    owner = block_columns // blocks_per_device
    xs, ys, cores = ROW_PARTS
    core = (owner - row_id) % cores
    shift_y = (owner // cores - row_id // cores) % ys
    shift_x = (owner // (cores * ys) - row_id // (cores * ys)) % xs
    piece = sum(
        jnp.where((shift_x == x) & (shift_y == y), index, 0) for index, (x, y) in enumerate(SHIFTS)
    )
    return (core * len(SHIFTS) + piece) * blocks_per_device + block_columns % blocks_per_device


def product_kernel(columns, values, gathered, *refs):
    *earlier, out, held, arrived = refs
    rows, count, order, _ = values.shape

    def fetch(row):
        return pltpu.make_async_copy(values.at[row], held.at[row], arrived.at[row])

    for row in range(rows):
        fetch(row).start()

    def one_row(row, carry):
        fetch(row).wait()
        total = None
        for k in range(count):
            column = pl.multiple_of(columns[row * count + k] * order, order)
            term = jnp.dot(
                held[row, k], gathered[pl.ds(column, order), :], preferred_element_type=jnp.float32
            )
            total = term if total is None else total + term
        own_rows = pl.ds(pl.multiple_of(row * order, order), order)
        for product in earlier:
            total = total - product[own_rows, :]
        out[own_rows, :] = total.astype(out.dtype)
        return carry

    lax.fori_loop(0, rows, one_row, 0)


def block_product(block_values, columns, gathered, *earlier):
    rows, count, order, _ = block_values.shape
    load_cases = gathered.shape[1]
    vmem = pl.BlockSpec(memory_space=pltpu.VMEM)
    return pl.pallas_call(
        product_kernel,
        out_shape=jax.ShapeDtypeStruct(
            (rows * order, load_cases), jnp.bfloat16 if earlier else jnp.float32
        ),
        in_specs=[
            pl.BlockSpec(memory_space=pltpu.SMEM),
            pl.BlockSpec(memory_space=pl.ANY),
            vmem,
            *[vmem] * len(earlier),
        ],
        out_specs=vmem,
        scratch_shapes=[
            pltpu.VMEM((rows, count, order, order), jnp.bfloat16),
            pltpu.SemaphoreType.DMA((rows,)),
        ],
        compiler_params=pltpu.CompilerParams(vmem_limit_bytes=48 * 1024 * 1024),
        cost_estimate=pl.CostEstimate(
            flops=2 * rows * count * order * order * load_cases,
            bytes_accessed=2 * rows * count * order * order,
            transcendentals=0,
        ),
    )(columns, block_values, gathered, *earlier)


def reduce_coefficients(sub_diag, main_diag, super_diag):
    factors = []
    for exponent in range(LEVELS):
        stride = 2**exponent
        lower_factor = -sub_diag / jnp.roll(main_diag, stride, 0)
        upper_factor = -super_diag / jnp.roll(main_diag, -stride, 0)
        factors.append((lower_factor, upper_factor))
        sub_diag, main_diag, super_diag = (
            lower_factor * jnp.roll(sub_diag, stride, 0),
            main_diag
            + lower_factor * jnp.roll(super_diag, stride, 0)
            + upper_factor * jnp.roll(sub_diag, -stride, 0),
            upper_factor * jnp.roll(super_diag, -stride, 0),
        )
    return factors, main_diag


def apply_reduction(factors, reduced, right_side):
    for exponent in range(LEVELS):
        stride = 2**exponent
        lower_factor, upper_factor = factors[exponent]
        right_side = (
            right_side
            + lower_factor * jnp.roll(right_side, stride, 0)
            + upper_factor * jnp.roll(right_side, -stride, 0)
        )
    return right_side / reduced


def shards(
    cosine_load,
    sine_load,
    base_stiffness,
    coupling_ratio,
    mistuning,
    sector_class,
    engine_order,
    block_values,
    block_columns,
):
    sectors = lax.axis_size("sector")
    sector_id = lax.axis_index("sector")
    local_rows, load_cases = cosine_load.shape
    slice_rows = local_rows // sectors
    order = block_values.shape[-1]

    def swap(cells):
        return lax.all_to_all(cells, "sector", 0, 0, tiled=True)

    def own_slice(cells, axis):
        return lax.dynamic_slice_in_dim(cells, sector_id * slice_rows, slice_rows, axis)

    all_classes = swap(jnp.broadcast_to(sector_class[:, None], (sectors, 1)))
    turns = (engine_order[0] * jnp.arange(sectors, dtype=jnp.int32)) % sectors
    angle = turns.astype(jnp.float32) * (2.0 * math.pi / sectors)
    cosine, sine = jnp.cos(angle)[:, None], jnp.sin(angle)[:, None]

    classes = mistuning.shape[0]
    picked = sum(
        jnp.where(all_classes == index, mistuning[index][None], 0.0) for index in range(classes)
    )
    diagonal = base_stiffness[None] * (1.0 + picked)
    coupling = coupling_ratio * base_stiffness
    cycle = jnp.broadcast_to(-coupling[None], diagonal.shape)
    factors, reduced = reduce_coefficients(cycle, diagonal, cycle)
    cosine_gain = apply_reduction(factors, reduced, jnp.broadcast_to(cosine, diagonal.shape))
    sine_gain = apply_reduction(factors, reduced, jnp.broadcast_to(sine, diagonal.shape))

    own_cosine = lax.dynamic_index_in_dim(cosine_gain, sector_id, 0, keepdims=False)
    own_sine = lax.dynamic_index_in_dim(sine_gain, sector_id, 0, keepdims=False)
    rounded = (own_cosine[:, None] * cosine_load + own_sine[:, None] * sine_load).astype(
        jnp.bfloat16
    )

    cosine_slice, sine_slice = own_slice(cosine_load, 0)[None], own_slice(sine_load, 0)[None]

    def spread(cells):
        return own_slice(cells, 1)[:, :, None]

    slice_factors = [(spread(lower), spread(upper)) for lower, upper in factors]
    slice_reduced, slice_diagonal = spread(reduced), spread(diagonal)
    slice_coupling = own_slice(coupling, 0)[None, :, None]
    forcing = cosine[:, :, None] * cosine_slice + sine[:, :, None] * sine_slice
    current = spread(cosine_gain) * cosine_slice + spread(sine_gain) * sine_slice

    columns = relative_columns(block_columns, block_values.shape[1]).reshape(-1)
    for iteration in range(1, ITERS):
        last = iteration == ITERS - 1
        gathered = gather_pieces(rounded)
        if last:
            change = block_product(block_values[0], columns, gathered, product)
            change = swap(change.reshape(sectors, slice_rows, load_cases))
            slice_product = slice_product + change.astype(jnp.float32)
        else:
            product = block_product(block_values[0], columns, gathered)
            slice_product = swap(product.reshape(sectors, slice_rows, load_cases))
        neighbours = jnp.roll(current, 1, 0) + jnp.roll(current, -1, 0)
        residual = forcing - (
            slice_diagonal * current - slice_coupling * neighbours + slice_product
        )
        sent = current.astype(jnp.bfloat16).astype(jnp.float32)
        current = current + apply_reduction(slice_factors, slice_reduced, residual)
        if not last:
            rounded = swap(current.astype(jnp.bfloat16)).reshape(local_rows, load_cases)
    difference = swap((current - sent).astype(jnp.bfloat16)).reshape(local_rows, load_cases)
    return (rounded.astype(jnp.float32) + difference.astype(jnp.float32))[None]


def solution(mesh):
    return jax.shard_map(
        shards,
        mesh=mesh,
        in_specs=(
            P("row", None),
            P("row", None),
            P("row"),
            P("row"),
            P(None, "row"),
            P("sector"),
            P(),
            P("sector", "row", None, None, None),
            P("row", None),
        ),
        out_specs=P("sector", "row", None),
        check_vma=False,
    )
```

```python
import functools
import math

import jax
import jax.numpy as jnp
from jax import lax
from jax.experimental import pallas as pl
from jax.experimental.pallas import tpu as pltpu
from jax.sharding import PartitionSpec as P

ITERS = 4
LEVELS = 3
ROW_PARTS = (2, 4, 2)


def row_peers(shift_x, shift_y, shift_core):
    pairs = []
    for x in range(ROW_PARTS[0]):
        for y in range(ROW_PARTS[1]):
            for core in range(ROW_PARTS[2]):
                source = (
                    ((x + shift_x) % ROW_PARTS[0] * ROW_PARTS[1] + (y + shift_y) % ROW_PARTS[1])
                    * ROW_PARTS[2]
                    + (core + shift_core) % ROW_PARTS[2]
                )
                target = (x * ROW_PARTS[1] + y) * ROW_PARTS[2] + core
                pairs.append((source, target))
    return pairs


SHIFTS = ((0, 0), (1, 0), (0, 2), (0, 1), (0, 3), (1, 1), (1, 3), (1, 2))


def gather_pieces(own):
    def fetch(block, *shift):
        return lax.ppermute(block, "row", row_peers(*shift))

    across = fetch(own, 1, 0, 0)
    opposite, above, below = fetch(own, 0, 2, 0), fetch(own, 0, 1, 0), fetch(own, 0, 3, 0)
    relayed = [fetch(across, 0, 1, 0), fetch(across, 0, 3, 0), fetch(opposite, 1, 0, 0)]
    direct = [own, across, opposite, above, below]
    order = direct + relayed
    swapped = [
        fetch(jnp.concatenate(part, axis=0), 0, 0, 1) for part in (order[:4], order[4:])
    ]
    return jnp.concatenate(direct + relayed + swapped, axis=0)


def relative_columns(block_columns, blocks_per_device):
    row_id = lax.axis_index("row")
    owner = block_columns // blocks_per_device
    xs, ys, cores = ROW_PARTS
    core = (owner - row_id) % cores
    shift_y = (owner // cores - row_id // cores) % ys
    shift_x = (owner // (cores * ys) - row_id // (cores * ys)) % xs
    piece = sum(
        jnp.where((shift_x == x) & (shift_y == y), index, 0) for index, (x, y) in enumerate(SHIFTS)
    )
    return (core * len(SHIFTS) + piece) * blocks_per_device + block_columns % blocks_per_device


def product_kernel(columns, values, gathered, *refs):
    *earlier, out = refs
    rows, count, order, _ = values.shape

    def one_row(row, carry):
        total = None
        for k in range(count):
            column = pl.multiple_of(columns[row * count + k] * order, order)
            term = jnp.dot(
                values[row, k], gathered[pl.ds(column, order), :], preferred_element_type=jnp.float32
            )
            total = term if total is None else total + term
        own_rows = pl.ds(pl.multiple_of(row * order, order), order)
        for product in earlier:
            total = total - product[own_rows, :]
        out[own_rows, :] = total.astype(out.dtype)
        return carry

    lax.fori_loop(0, rows, one_row, 0)


def block_product(block_values, columns, gathered, *earlier):
    rows, count, order, _ = block_values.shape
    load_cases = gathered.shape[1]
    vmem = pl.BlockSpec(memory_space=pltpu.VMEM)
    return pl.pallas_call(
        product_kernel,
        out_shape=jax.ShapeDtypeStruct(
            (rows * order, load_cases), jnp.bfloat16 if earlier else jnp.float32
        ),
        in_specs=[
            pl.BlockSpec(memory_space=pltpu.SMEM),
            vmem,
            vmem,
            *[vmem] * len(earlier),
        ],
        out_specs=vmem,
        compiler_params=pltpu.CompilerParams(vmem_limit_bytes=16 * 1024 * 1024),
        cost_estimate=pl.CostEstimate(
            flops=2 * rows * count * order * order * load_cases,
            bytes_accessed=2 * rows * count * order * order,
            transcendentals=0,
        ),
    )(columns, block_values, gathered, *earlier)


def shifted(cells, distance):
    return [cells[(sector - distance) % len(cells)] for sector in range(len(cells))]


def reduce_coefficients(sub_diag, main_diag, super_diag):
    factors = []
    for exponent in range(LEVELS):
        stride = 2**exponent
        lower = [-a / b for a, b in zip(sub_diag, shifted(main_diag, stride))]
        upper = [-a / b for a, b in zip(super_diag, shifted(main_diag, -stride))]
        factors.append((lower, upper))
        sub_diag, main_diag, super_diag = (
            [a * b for a, b in zip(lower, shifted(sub_diag, stride))],
            [
                main + a * b + c * d
                for main, a, b, c, d in zip(
                    main_diag,
                    lower,
                    shifted(super_diag, stride),
                    upper,
                    shifted(sub_diag, -stride),
                )
            ],
            [a * b for a, b in zip(upper, shifted(super_diag, -stride))],
        )
    return factors, main_diag


def apply_reduction(factors, reduced, right_side):
    for exponent in range(LEVELS):
        stride = 2**exponent
        lower, upper = factors[exponent]
        right_side = [
            own + a * below + b * above
            for own, a, below, b, above in zip(
                right_side,
                lower,
                shifted(right_side, stride),
                upper,
                shifted(right_side, -stride),
            )
        ]
    return [a / b for a, b in zip(right_side, reduced)]


GAINS = 2 * LEVELS
REDUCED, DIAGONAL, COUPLING, KINDS = GAINS + 2, GAINS + 3, GAINS + 4, GAINS + 5


def coefficient_kernel(
    classes, own, cosine, sine, mistuning, base, ratio, cosine_load, sine_load, rounded, table
):
    sectors = table.shape[1]
    stiffness = base[...]
    coupling = ratio[...] * stiffness
    diagonal = [stiffness * (1.0 + mistuning[classes[s]]) for s in range(sectors)]
    factors, reduced = reduce_coefficients([-coupling] * sectors, diagonal, [-coupling] * sectors)
    gains = [
        apply_reduction(
            factors, reduced, [jnp.full(stiffness.shape, wave[s], jnp.float32) for s in range(sectors)]
        )
        for wave in (cosine, sine)
    ]
    kinds = [part for pair in factors for part in pair]
    kinds += [*gains, reduced, diagonal, [coupling] * sectors]
    for kind, cells in enumerate(kinds):
        for s in range(sectors):
            table[kind, s] = cells[s]
    groups, lanes = stiffness.shape
    cosine_gain, sine_gain = table[GAINS, own[0]].T, table[GAINS + 1, own[0]].T
    for group in range(groups):
        rows = pl.ds(group * lanes, lanes)
        rounded[rows, :] = (
            cosine_gain[:, group : group + 1] * cosine_load[rows, :]
            + sine_gain[:, group : group + 1] * sine_load[rows, :]
        ).astype(rounded.dtype)


def sector_kernel(last, cosine, sine, table, cosine_load, sine_load, current, *refs):
    products, outs = (refs[:2], refs[2:]) if last else (refs[:1], refs[1:])
    sectors, rows, _ = current.shape
    step = 16

    def one_group(group, carry):
        at = pl.ds(pl.multiple_of(group * step, step), step)
        wave_c, wave_s = cosine_load[at, :], sine_load[at, :]
        before = [current[s, at, :] for s in range(sectors)]
        below, above = shifted(before, 1), shifted(before, -1)
        residual = []
        for s in range(sectors):
            forcing = cosine[s] * wave_c + sine[s] * wave_s
            product = sum(part[s, at, :].astype(jnp.float32) for part in products)
            applied = (
                table[DIAGONAL, s, at, :] * before[s]
                - table[COUPLING, s, at, :] * (below[s] + above[s])
                + product
            )
            residual.append(forcing - applied)
        factors = [
            tuple([table[2 * level + side, s, at, :] for s in range(sectors)] for side in range(2))
            for level in range(LEVELS)
        ]
        reduced = [table[REDUCED, s, at, :] for s in range(sectors)]
        correction = apply_reduction(factors, reduced, residual)
        for s in range(sectors):
            after = before[s] + correction[s]
            if last:
                sent = before[s].astype(jnp.bfloat16).astype(jnp.float32)
                outs[0][s, at, :] = (after - sent).astype(jnp.bfloat16)
            else:
                outs[0][s, at, :] = after.astype(jnp.bfloat16)
                outs[1][s, at, :] = after
        return carry

    lax.fori_loop(0, rows // step, one_group, 0)


def shards(
    cosine_load,
    sine_load,
    base_stiffness,
    coupling_ratio,
    mistuning,
    sector_class,
    engine_order,
    block_values,
    block_columns,
):
    sectors = lax.axis_size("sector")
    sector_id = lax.axis_index("sector")
    local_rows, load_cases = cosine_load.shape
    slice_rows = local_rows // sectors
    smem, vmem = (pl.BlockSpec(memory_space=space) for space in (pltpu.SMEM, pltpu.VMEM))

    def swap(cells):
        return lax.all_to_all(cells, "sector", 0, 0, tiled=True)

    def own_slice(cells, axis):
        return lax.dynamic_slice_in_dim(cells, sector_id * slice_rows, slice_rows, axis)

    all_classes = swap(jnp.broadcast_to(sector_class[:, None], (sectors, 1))).reshape(-1)
    turns = (engine_order[0] * jnp.arange(sectors, dtype=jnp.int32)) % sectors
    angle = turns.astype(jnp.float32) * (2.0 * math.pi / sectors)
    cosine, sine = jnp.cos(angle), jnp.sin(angle)

    lanes = 128
    groups = local_rows // lanes
    rounded, table = pl.pallas_call(
        coefficient_kernel,
        out_shape=(
            jax.ShapeDtypeStruct((local_rows, load_cases), jnp.bfloat16),
            jax.ShapeDtypeStruct((KINDS, sectors, groups, lanes), jnp.float32),
        ),
        in_specs=[smem] * 4 + [vmem] * 5,
        out_specs=(vmem, vmem),
        compiler_params=pltpu.CompilerParams(vmem_limit_bytes=16 * 1024 * 1024),
    )(
        all_classes,
        sector_id[None],
        cosine,
        sine,
        mistuning.reshape(-1, groups, lanes),
        base_stiffness.reshape(groups, lanes),
        coupling_ratio.reshape(groups, lanes),
        cosine_load,
        sine_load,
    )

    cosine_slice, sine_slice = own_slice(cosine_load, 0), own_slice(sine_load, 0)
    table = own_slice(table.reshape(KINDS * sectors, local_rows), 1)
    table = jnp.broadcast_to(
        table.reshape(KINDS, sectors, slice_rows, 1), (KINDS, sectors, slice_rows, load_cases)
    )
    current = table[GAINS] * cosine_slice + table[GAINS + 1] * sine_slice

    columns = relative_columns(block_columns, block_values.shape[1]).reshape(-1)
    slice_shape = (sectors, slice_rows, load_cases)
    products = []
    for iteration in range(1, ITERS):
        last = iteration == ITERS - 1
        gathered = gather_pieces(rounded)
        if last:
            change = block_product(block_values[0], columns, gathered, product)
            products.append(swap(change.reshape(slice_shape)))
        else:
            product = block_product(block_values[0], columns, gathered)
            products = [swap(product.reshape(slice_shape))]
        outs = [jax.ShapeDtypeStruct(slice_shape, jnp.bfloat16)]
        if not last:
            outs.append(jax.ShapeDtypeStruct(slice_shape, jnp.float32))
        outs = pl.pallas_call(
            functools.partial(sector_kernel, last),
            out_shape=outs,
            in_specs=[smem] * 2 + [vmem] * (4 + len(products)),
            out_specs=[vmem] * len(outs),
            compiler_params=pltpu.CompilerParams(vmem_limit_bytes=16 * 1024 * 1024),
        )(cosine, sine, table, cosine_slice, sine_slice, current, *products)
        received = swap(outs[0]).reshape(local_rows, load_cases)
        if last:
            return (rounded.astype(jnp.float32) + received.astype(jnp.float32))[None]
        rounded, current = received, outs[1]


def solution(mesh):
    return jax.shard_map(
        shards,
        mesh=mesh,
        in_specs=(
            P("row", None),
            P("row", None),
            P("row"),
            P("row"),
            P(None, "row"),
            P("sector"),
            P(),
            P("sector", "row", None, None, None),
            P("row", None),
        ),
        out_specs=P("sector", "row", None),
        check_vma=False,
    )
```

```python
import functools
import math

import jax
import jax.numpy as jnp
from jax import lax
from jax.experimental import pallas as pl
from jax.experimental.pallas import tpu as pltpu
from jax.sharding import PartitionSpec as P

ITERS = 4
LEVELS = 3
ROW_PARTS = (2, 4, 2)


def row_peers(shift_x, shift_y, shift_core):
    pairs = []
    for x in range(ROW_PARTS[0]):
        for y in range(ROW_PARTS[1]):
            for core in range(ROW_PARTS[2]):
                source = (
                    ((x + shift_x) % ROW_PARTS[0] * ROW_PARTS[1] + (y + shift_y) % ROW_PARTS[1])
                    * ROW_PARTS[2]
                    + (core + shift_core) % ROW_PARTS[2]
                )
                target = (x * ROW_PARTS[1] + y) * ROW_PARTS[2] + core
                pairs.append((source, target))
    return pairs


SHIFTS = ((0, 0), (1, 0), (0, 2), (0, 1), (0, 3), (1, 1), (1, 3), (1, 2))


def gather_pieces(own, riders=()):
    def fetch(block, *shift):
        return lax.ppermute(block, "row", row_peers(*shift))

    across = fetch(own, 1, 0, 0)
    opposite, above, below = fetch(own, 0, 2, 0), fetch(own, 0, 1, 0), fetch(own, 0, 3, 0)
    relayed = [fetch(across, 0, 1, 0), fetch(across, 0, 3, 0), fetch(opposite, 1, 0, 0)]
    direct = [own, across, opposite, above, below]
    order = direct + relayed
    early, late = (jnp.concatenate(part, axis=0) for part in (order[:4], order[4:]))
    early, riders = lax.optimization_barrier((early, riders))
    swapped = [fetch(part, 0, 0, 1) for part in (early, late)]
    return jnp.concatenate(order + swapped, axis=0), riders


def relative_columns(block_columns, blocks_per_device):
    row_id = lax.axis_index("row")
    owner = block_columns // blocks_per_device
    xs, ys, cores = ROW_PARTS
    core = (owner - row_id) % cores
    shift_y = (owner // cores - row_id // cores) % ys
    shift_x = (owner // (cores * ys) - row_id // (cores * ys)) % xs
    piece = sum(
        jnp.where((shift_x == x) & (shift_y == y), index, 0) for index, (x, y) in enumerate(SHIFTS)
    )
    return (core * len(SHIFTS) + piece) * blocks_per_device + block_columns % blocks_per_device


def product_kernel(columns, values, gathered, *refs):
    *earlier, out = refs
    rows, count, order, _ = values.shape

    def one_row(row, carry):
        total = None
        for k in range(count):
            column = pl.multiple_of(columns[row * count + k] * order, order)
            term = jnp.dot(
                values[row, k], gathered[pl.ds(column, order), :], preferred_element_type=jnp.float32
            )
            total = term if total is None else total + term
        own_rows = pl.ds(pl.multiple_of(row * order, order), order)
        for product in earlier:
            total = total - product[own_rows, :]
        out[own_rows, :] = total.astype(out.dtype)
        return carry

    lax.fori_loop(0, rows, one_row, 0)


def block_product(block_values, columns, gathered, *earlier):
    rows, count, order, _ = block_values.shape
    load_cases = gathered.shape[1]
    vmem = pl.BlockSpec(memory_space=pltpu.VMEM)
    return pl.pallas_call(
        product_kernel,
        out_shape=jax.ShapeDtypeStruct(
            (rows * order, load_cases), jnp.bfloat16 if earlier else jnp.float32
        ),
        in_specs=[
            pl.BlockSpec(memory_space=pltpu.SMEM),
            vmem,
            vmem,
            *[vmem] * len(earlier),
        ],
        out_specs=vmem,
        compiler_params=pltpu.CompilerParams(vmem_limit_bytes=16 * 1024 * 1024),
        cost_estimate=pl.CostEstimate(
            flops=2 * rows * count * order * order * load_cases,
            bytes_accessed=2 * rows * count * order * order,
            transcendentals=0,
        ),
    )(columns, block_values, gathered, *earlier)


def shifted(cells, distance):
    return [cells[(sector - distance) % len(cells)] for sector in range(len(cells))]


def reduce_coefficients(sub_diag, main_diag, super_diag):
    factors = []
    for exponent in range(LEVELS):
        stride = 2**exponent
        lower = [-a / b for a, b in zip(sub_diag, shifted(main_diag, stride))]
        upper = [-a / b for a, b in zip(super_diag, shifted(main_diag, -stride))]
        factors.append((lower, upper))
        sub_diag, main_diag, super_diag = (
            [a * b for a, b in zip(lower, shifted(sub_diag, stride))],
            [
                main + a * b + c * d
                for main, a, b, c, d in zip(
                    main_diag,
                    lower,
                    shifted(super_diag, stride),
                    upper,
                    shifted(sub_diag, -stride),
                )
            ],
            [a * b for a, b in zip(upper, shifted(super_diag, -stride))],
        )
    return factors, main_diag


def apply_reduction(factors, reduced, right_side):
    for exponent in range(LEVELS):
        stride = 2**exponent
        lower, upper = factors[exponent]
        right_side = [
            own + a * below + b * above
            for own, a, below, b, above in zip(
                right_side,
                lower,
                shifted(right_side, stride),
                upper,
                shifted(right_side, -stride),
            )
        ]
    return [a / b for a, b in zip(right_side, reduced)]


GAINS = 2 * LEVELS
REDUCED, DIAGONAL, COUPLING, KINDS = GAINS + 2, GAINS + 3, GAINS + 4, GAINS + 5


def coefficient_kernel(
    classes, own, cosine, sine, diagonals, couplings, loads, more_loads, rounded, table, held, arrived
):
    copies = [
        pltpu.make_async_copy(source, held.at[side], arrived.at[side])
        for side, source in enumerate((loads, more_loads))
    ]
    for copy in copies:
        copy.start()
    sectors = table.shape[1]
    coupling = couplings[...]
    diagonal = [diagonals[classes[s]] for s in range(sectors)]
    factors, reduced = reduce_coefficients([-coupling] * sectors, diagonal, [-coupling] * sectors)
    gains = [
        apply_reduction(
            factors, reduced, [jnp.full(coupling.shape, wave[s], jnp.float32) for s in range(sectors)]
        )
        for wave in (cosine, sine)
    ]
    kinds = [part for pair in factors for part in pair]
    kinds += [*gains, reduced, diagonal, [coupling] * sectors]
    for kind, cells in enumerate(kinds):
        for s in range(sectors):
            table[kind, s] = cells[s]
    groups, lanes = coupling.shape
    cosine_gain, sine_gain = table[GAINS, own[0]].T, table[GAINS + 1, own[0]].T
    for copy in copies:
        copy.wait()
    for group in range(groups):
        rows = pl.ds(group * lanes, lanes)
        rounded[rows, :] = (
            cosine_gain[:, group : group + 1] * held[0, rows, :]
            + sine_gain[:, group : group + 1] * held[1, rows, :]
        ).astype(rounded.dtype)


def sector_kernel(last, cosine, sine, table, cosine_load, sine_load, current, *refs):
    products, outs = (refs[:2], refs[2:]) if last else (refs[:1], refs[1:])
    sectors, rows, _ = current.shape
    step = 16

    def one_group(group, carry):
        at = pl.ds(pl.multiple_of(group * step, step), step)
        wave_c, wave_s = cosine_load[at, :], sine_load[at, :]
        before = [current[s, at, :] for s in range(sectors)]
        below, above = shifted(before, 1), shifted(before, -1)
        residual = []
        for s in range(sectors):
            forcing = cosine[s] * wave_c + sine[s] * wave_s
            product = sum(part[s, at, :].astype(jnp.float32) for part in products)
            applied = (
                table[DIAGONAL, s, at, :] * before[s]
                - table[COUPLING, s, at, :] * (below[s] + above[s])
                + product
            )
            residual.append(forcing - applied)
        factors = [
            tuple([table[2 * level + side, s, at, :] for s in range(sectors)] for side in range(2))
            for level in range(LEVELS)
        ]
        reduced = [table[REDUCED, s, at, :] for s in range(sectors)]
        correction = apply_reduction(factors, reduced, residual)
        for s in range(sectors):
            after = before[s] + correction[s]
            if last:
                sent = before[s].astype(jnp.bfloat16).astype(jnp.float32)
                outs[0][s, at, :] = (after - sent).astype(jnp.bfloat16)
            else:
                outs[0][s, at, :] = after.astype(jnp.bfloat16)
                outs[1][s, at, :] = after
        return carry

    lax.fori_loop(0, rows // step, one_group, 0)


def shards(
    cosine_load,
    sine_load,
    base_stiffness,
    coupling_ratio,
    mistuning,
    sector_class,
    engine_order,
    block_values,
    block_columns,
):
    sectors = lax.axis_size("sector")
    sector_id = lax.axis_index("sector")
    local_rows, load_cases = cosine_load.shape
    slice_rows = local_rows // sectors
    smem, vmem = (pl.BlockSpec(memory_space=space) for space in (pltpu.SMEM, pltpu.VMEM))

    def swap(cells):
        return lax.all_to_all(cells, "sector", 0, 0, tiled=True)

    def own_slice(cells, axis):
        return lax.dynamic_slice_in_dim(cells, sector_id * slice_rows, slice_rows, axis)

    all_classes = swap(jnp.broadcast_to(sector_class[:, None], (sectors, 1))).reshape(-1)
    turns = (engine_order[0] * jnp.arange(sectors, dtype=jnp.int32)) % sectors
    angle = turns.astype(jnp.float32) * (2.0 * math.pi / sectors)
    cosine, sine = jnp.cos(angle), jnp.sin(angle)

    lanes = 128
    groups = local_rows // lanes
    base = base_stiffness.reshape(groups, lanes)
    coupling = coupling_ratio.reshape(groups, lanes) * base
    diagonals = base * (1.0 + mistuning.reshape(-1, groups, lanes))
    rounded, table = pl.pallas_call(
        coefficient_kernel,
        out_shape=(
            jax.ShapeDtypeStruct((local_rows, load_cases), jnp.bfloat16),
            jax.ShapeDtypeStruct((KINDS, sectors, groups, lanes), jnp.float32),
        ),
        in_specs=[smem] * 4 + [vmem] * 2 + [pl.BlockSpec(memory_space=pl.ANY)] * 2,
        out_specs=(vmem, vmem),
        scratch_shapes=[
            pltpu.VMEM((2, local_rows, load_cases), jnp.float32),
            pltpu.SemaphoreType.DMA((2,)),
        ],
        compiler_params=pltpu.CompilerParams(vmem_limit_bytes=58 * 1024 * 1024),
    )(
        all_classes,
        sector_id[None],
        cosine,
        sine,
        diagonals,
        coupling,
        cosine_load,
        sine_load,
    )

    cosine_slice, sine_slice = own_slice(cosine_load, 0), own_slice(sine_load, 0)
    table = own_slice(table.reshape(KINDS * sectors, local_rows), 1)
    table = jnp.broadcast_to(
        table.reshape(KINDS, sectors, slice_rows, 1), (KINDS, sectors, slice_rows, load_cases)
    )
    current = table[GAINS] * cosine_slice + table[GAINS + 1] * sine_slice

    columns = relative_columns(block_columns, block_values.shape[1]).reshape(-1)
    slice_shape = (sectors, slice_rows, load_cases)
    products = []
    for iteration in range(1, ITERS):
        last = iteration == ITERS - 1
        gathered, (table, current) = gather_pieces(rounded, (table, current))
        if last:
            change = block_product(block_values[0], columns, gathered, product)
            products.append(swap(change.reshape(slice_shape)))
        else:
            product = block_product(block_values[0], columns, gathered)
            products = [swap(product.reshape(slice_shape))]
        outs = [jax.ShapeDtypeStruct(slice_shape, jnp.bfloat16)]
        if not last:
            outs.append(jax.ShapeDtypeStruct(slice_shape, jnp.float32))
        outs = pl.pallas_call(
            functools.partial(sector_kernel, last),
            out_shape=outs,
            in_specs=[smem] * 2 + [vmem] * (4 + len(products)),
            out_specs=[vmem] * len(outs),
            compiler_params=pltpu.CompilerParams(vmem_limit_bytes=16 * 1024 * 1024),
        )(cosine, sine, table, cosine_slice, sine_slice, current, *products)
        received = swap(outs[0]).reshape(local_rows, load_cases)
        if last:
            return (rounded.astype(jnp.float32) + received.astype(jnp.float32))[None]
        rounded, current = received, outs[1]


def solution(mesh):
    return jax.shard_map(
        shards,
        mesh=mesh,
        in_specs=(
            P("row", None),
            P("row", None),
            P("row"),
            P("row"),
            P(None, "row"),
            P("sector"),
            P(),
            P("sector", "row", None, None, None),
            P("row", None),
        ),
        out_specs=P("sector", "row", None),
        check_vma=False,
    )
```

```python
import functools
import math

import jax
import jax.numpy as jnp
from jax import lax
from jax.experimental import pallas as pl
from jax.experimental.pallas import tpu as pltpu
from jax.sharding import PartitionSpec as P

ITERS = 4
LEVELS = 3
ROW_PARTS = (2, 4, 2)


def row_peers(shift_x, shift_y, shift_core):
    pairs = []
    for x in range(ROW_PARTS[0]):
        for y in range(ROW_PARTS[1]):
            for core in range(ROW_PARTS[2]):
                source = (
                    ((x + shift_x) % ROW_PARTS[0] * ROW_PARTS[1] + (y + shift_y) % ROW_PARTS[1])
                    * ROW_PARTS[2]
                    + (core + shift_core) % ROW_PARTS[2]
                )
                target = (x * ROW_PARTS[1] + y) * ROW_PARTS[2] + core
                pairs.append((source, target))
    return pairs


SHIFTS = ((0, 0), (1, 0), (0, 2), (0, 1), (0, 3), (1, 1), (1, 3), (1, 2))


def joined(blocks):
    half = blocks[0].shape[0] // 2
    return jnp.concatenate([blocks[0][:half], blocks[0][half:], *blocks[1:]], axis=0)


def gather_pieces(own, riders=()):
    def fetch(block, *shift):
        return lax.ppermute(block, "row", row_peers(*shift))

    across = fetch(own, 1, 0, 0)
    opposite, above, below = fetch(own, 0, 2, 0), fetch(own, 0, 1, 0), fetch(own, 0, 3, 0)
    relayed = [fetch(across, 0, 1, 0), fetch(across, 0, 3, 0), fetch(opposite, 1, 0, 0)]
    direct = [own, across, opposite, above, below]
    order = direct + relayed
    early, late = (joined(part) for part in (order[:4], order[4:]))
    early, riders = lax.optimization_barrier((early, riders))
    swapped = [fetch(part, 0, 0, 1) for part in (early, late)]
    return jnp.concatenate(order + swapped, axis=0), riders


def relative_columns(block_columns, blocks_per_device):
    row_id = lax.axis_index("row")
    owner = block_columns // blocks_per_device
    xs, ys, cores = ROW_PARTS
    core = (owner - row_id) % cores
    shift_y = (owner // cores - row_id // cores) % ys
    shift_x = (owner // (cores * ys) - row_id // (cores * ys)) % xs
    piece = sum(
        jnp.where((shift_x == x) & (shift_y == y), index, 0) for index, (x, y) in enumerate(SHIFTS)
    )
    return (core * len(SHIFTS) + piece) * blocks_per_device + block_columns % blocks_per_device


def product_kernel(columns, values, gathered, *refs):
    *earlier, out = refs
    rows, count, order, _ = values.shape

    def one_row(row, carry):
        total = None
        for k in range(count):
            column = pl.multiple_of(columns[row * count + k] * order, order)
            term = jnp.dot(
                values[row, k], gathered[pl.ds(column, order), :], preferred_element_type=jnp.float32
            )
            total = term if total is None else total + term
        own_rows = pl.ds(pl.multiple_of(row * order, order), order)
        for product in earlier:
            total = total - product[own_rows, :]
        out[own_rows, :] = total.astype(out.dtype)
        return carry

    lax.fori_loop(0, rows, one_row, 0)


def block_product(block_values, columns, gathered, *earlier):
    rows, count, order, _ = block_values.shape
    load_cases = gathered.shape[1]
    vmem = pl.BlockSpec(memory_space=pltpu.VMEM)
    return pl.pallas_call(
        product_kernel,
        out_shape=jax.ShapeDtypeStruct(
            (rows * order, load_cases), jnp.bfloat16 if earlier else jnp.float32
        ),
        in_specs=[
            pl.BlockSpec(memory_space=pltpu.SMEM),
            vmem,
            vmem,
            *[vmem] * len(earlier),
        ],
        out_specs=vmem,
        compiler_params=pltpu.CompilerParams(vmem_limit_bytes=16 * 1024 * 1024),
        cost_estimate=pl.CostEstimate(
            flops=2 * rows * count * order * order * load_cases,
            bytes_accessed=2 * rows * count * order * order,
            transcendentals=0,
        ),
    )(columns, block_values, gathered, *earlier)


def shifted(cells, distance):
    return [cells[(sector - distance) % len(cells)] for sector in range(len(cells))]


def reduce_coefficients(sub_diag, main_diag, super_diag):
    factors = []
    for exponent in range(LEVELS):
        stride = 2**exponent
        lower = [-a / b for a, b in zip(sub_diag, shifted(main_diag, stride))]
        upper = [-a / b for a, b in zip(super_diag, shifted(main_diag, -stride))]
        factors.append((lower, upper))
        sub_diag, main_diag, super_diag = (
            [a * b for a, b in zip(lower, shifted(sub_diag, stride))],
            [
                main + a * b + c * d
                for main, a, b, c, d in zip(
                    main_diag,
                    lower,
                    shifted(super_diag, stride),
                    upper,
                    shifted(sub_diag, -stride),
                )
            ],
            [a * b for a, b in zip(upper, shifted(super_diag, -stride))],
        )
    return factors, main_diag


def apply_reduction(factors, reduced, right_side):
    for exponent in range(LEVELS):
        stride = 2**exponent
        lower, upper = factors[exponent]
        right_side = [
            own + a * below + b * above
            for own, a, below, b, above in zip(
                right_side,
                lower,
                shifted(right_side, stride),
                upper,
                shifted(right_side, -stride),
            )
        ]
    return [a / b for a, b in zip(right_side, reduced)]


GAINS = 2 * LEVELS
REDUCED, DIAGONAL, COUPLING, KINDS = GAINS + 2, GAINS + 3, GAINS + 4, GAINS + 5


def staging_kernel(cosine_load, sine_load, base, ratio, mistuning, loads, diagonals, couplings, *held):
    *held, arrived = held
    targets = (loads.at[0], loads.at[1], *held)
    copies = [
        pltpu.make_async_copy(source, target, arrived.at[index])
        for index, (source, target) in enumerate(
            zip((cosine_load, sine_load, base, ratio, mistuning), targets)
        )
    ]
    for copy in copies[::-1]:
        copy.start()
    for copy in copies[2:]:
        copy.wait()
    stiffness, spring, deviation = (part[...] for part in held)
    groups, lanes = stiffness.shape
    couplings[...] = spring * stiffness
    for index in range(deviation.shape[0]):
        rows = [
            deviation[index : index + 1, group * lanes : (group + 1) * lanes]
            for group in range(groups)
        ]
        diagonals[index] = stiffness * (1.0 + jnp.concatenate(rows, axis=0))
    for copy in copies[:2]:
        copy.wait()


def coefficient_kernel(classes, own, cosine, sine, diagonals, couplings, loads, rounded, table):
    sectors = table.shape[1]
    coupling = couplings[...]
    diagonal = [diagonals[classes[s]] for s in range(sectors)]
    factors, reduced = reduce_coefficients([-coupling] * sectors, diagonal, [-coupling] * sectors)
    gains = [
        apply_reduction(
            factors, reduced, [jnp.full(coupling.shape, wave[s], jnp.float32) for s in range(sectors)]
        )
        for wave in (cosine, sine)
    ]
    kinds = [part for pair in factors for part in pair]
    kinds += [*gains, reduced, diagonal, [coupling] * sectors]
    for kind, cells in enumerate(kinds):
        for s in range(sectors):
            table[kind, s] = cells[s]
    groups, lanes = coupling.shape
    cosine_gain, sine_gain = table[GAINS, own[0]].T, table[GAINS + 1, own[0]].T
    for group in range(groups):
        rows = pl.ds(group * lanes, lanes)
        rounded[rows, :] = (
            cosine_gain[:, group : group + 1] * loads[0, rows, :]
            + sine_gain[:, group : group + 1] * loads[1, rows, :]
        ).astype(rounded.dtype)


def sector_kernel(last, cosine, sine, table, cosine_load, sine_load, current, *refs):
    products, outs = (refs[:2], refs[2:]) if last else (refs[:1], refs[1:])
    sectors, rows, _ = current.shape
    step = 16

    def one_group(group, carry):
        at = pl.ds(pl.multiple_of(group * step, step), step)
        wave_c, wave_s = cosine_load[at, :], sine_load[at, :]
        before = [current[s, at, :] for s in range(sectors)]
        below, above = shifted(before, 1), shifted(before, -1)
        residual = []
        for s in range(sectors):
            forcing = cosine[s] * wave_c + sine[s] * wave_s
            product = sum(part[s, at, :].astype(jnp.float32) for part in products)
            applied = (
                table[DIAGONAL, s, at, :] * before[s]
                - table[COUPLING, s, at, :] * (below[s] + above[s])
                + product
            )
            residual.append(forcing - applied)
        factors = [
            tuple([table[2 * level + side, s, at, :] for s in range(sectors)] for side in range(2))
            for level in range(LEVELS)
        ]
        reduced = [table[REDUCED, s, at, :] for s in range(sectors)]
        correction = apply_reduction(factors, reduced, residual)
        for s in range(sectors):
            after = before[s] + correction[s]
            if last:
                sent = before[s].astype(jnp.bfloat16).astype(jnp.float32)
                outs[0][s, at, :] = (after - sent).astype(jnp.bfloat16)
            else:
                outs[0][s, at, :] = after.astype(jnp.bfloat16)
                outs[1][s, at, :] = after
        return carry

    lax.fori_loop(0, rows // step, one_group, 0)


def shards(
    cosine_load,
    sine_load,
    base_stiffness,
    coupling_ratio,
    mistuning,
    sector_class,
    engine_order,
    block_values,
    block_columns,
):
    sectors = lax.axis_size("sector")
    sector_id = lax.axis_index("sector")
    local_rows, load_cases = cosine_load.shape
    slice_rows = local_rows // sectors
    smem, vmem = (pl.BlockSpec(memory_space=space) for space in (pltpu.SMEM, pltpu.VMEM))

    def swap(cells):
        return lax.all_to_all(cells, "sector", 0, 0, tiled=True)

    def own_slice(cells, axis):
        return lax.dynamic_slice_in_dim(cells, sector_id * slice_rows, slice_rows, axis)

    all_classes = swap(jnp.broadcast_to(sector_class[:, None], (sectors, 1))).reshape(-1)
    turns = (engine_order[0] * jnp.arange(sectors, dtype=jnp.int32)) % sectors
    angle = turns.astype(jnp.float32) * (2.0 * math.pi / sectors)
    cosine, sine = jnp.cos(angle), jnp.sin(angle)

    lanes = 128
    groups = local_rows // lanes
    loads, diagonals, couplings = pl.pallas_call(
        staging_kernel,
        out_shape=(
            jax.ShapeDtypeStruct((2, local_rows, load_cases), jnp.float32),
            jax.ShapeDtypeStruct((mistuning.shape[0], groups, lanes), jnp.float32),
            jax.ShapeDtypeStruct((groups, lanes), jnp.float32),
        ),
        in_specs=[pl.BlockSpec(memory_space=pl.ANY)] * 5,
        out_specs=(vmem,) * 3,
        scratch_shapes=[
            pltpu.VMEM((groups, lanes), jnp.float32),
            pltpu.VMEM((groups, lanes), jnp.float32),
            pltpu.VMEM(mistuning.shape, jnp.float32),
            pltpu.SemaphoreType.DMA((5,)),
        ],
        compiler_params=pltpu.CompilerParams(vmem_limit_bytes=16 * 1024 * 1024),
    )(
        *[
            pltpu.with_memory_space_constraint(part, pltpu.HBM)
            for part in (
                cosine_load,
                sine_load,
                base_stiffness.reshape(groups, lanes),
                coupling_ratio.reshape(groups, lanes),
                mistuning,
            )
        ]
    )
    rounded, table = pl.pallas_call(
        coefficient_kernel,
        out_shape=(
            jax.ShapeDtypeStruct((local_rows, load_cases), jnp.bfloat16),
            jax.ShapeDtypeStruct((KINDS, sectors, groups, lanes), jnp.float32),
        ),
        in_specs=[smem] * 4 + [vmem] * 3,
        out_specs=(vmem, vmem),
        compiler_params=pltpu.CompilerParams(vmem_limit_bytes=16 * 1024 * 1024),
    )(all_classes, sector_id[None], cosine, sine, diagonals, couplings, loads)
    rounded, loads, block_columns = lax.optimization_barrier((rounded, loads, block_columns))

    cosine_slice, sine_slice = own_slice(loads[0], 0), own_slice(loads[1], 0)
    table = own_slice(table.reshape(KINDS * sectors, local_rows), 1)
    table = jnp.broadcast_to(
        table.reshape(KINDS, sectors, slice_rows, 1), (KINDS, sectors, slice_rows, load_cases)
    )
    current = table[GAINS] * cosine_slice + table[GAINS + 1] * sine_slice

    columns = relative_columns(block_columns, block_values.shape[1]).reshape(-1)
    slice_shape = (sectors, slice_rows, load_cases)
    products = []
    for iteration in range(1, ITERS):
        last = iteration == ITERS - 1
        gathered, (table, current) = gather_pieces(rounded, (table, current))
        if last:
            change = block_product(block_values[0], columns, gathered, product)
            products.append(swap(change.reshape(slice_shape)))
        else:
            product = block_product(block_values[0], columns, gathered)
            products = [swap(product.reshape(slice_shape))]
        outs = [jax.ShapeDtypeStruct(slice_shape, jnp.bfloat16)]
        if not last:
            outs.append(jax.ShapeDtypeStruct(slice_shape, jnp.float32))
        outs = pl.pallas_call(
            functools.partial(sector_kernel, last),
            out_shape=outs,
            in_specs=[smem] * 2 + [vmem] * (4 + len(products)),
            out_specs=[vmem] * len(outs),
            compiler_params=pltpu.CompilerParams(vmem_limit_bytes=16 * 1024 * 1024),
        )(cosine, sine, table, cosine_slice, sine_slice, current, *products)
        received = swap(outs[0]).reshape(local_rows, load_cases)
        if last:
            return (rounded.astype(jnp.float32) + received.astype(jnp.float32))[None]
        rounded, current = received, outs[1]


def solution(mesh):
    return jax.shard_map(
        shards,
        mesh=mesh,
        in_specs=(
            P("row", None),
            P("row", None),
            P("row"),
            P("row"),
            P(None, "row"),
            P("sector"),
            P(),
            P("sector", "row", None, None, None),
            P("row", None),
        ),
        out_specs=P("sector", "row", None),
        check_vma=False,
    )
```

```python
import functools
import math

import jax
import jax.numpy as jnp
from jax import lax
from jax.experimental import pallas as pl
from jax.experimental.pallas import tpu as pltpu
from jax.sharding import PartitionSpec as P

ITERS = 4
LEVELS = 3
ROW_PARTS = (2, 4, 2)


def row_peers(shift_x, shift_y, shift_core):
    pairs = []
    for x in range(ROW_PARTS[0]):
        for y in range(ROW_PARTS[1]):
            for core in range(ROW_PARTS[2]):
                source = (
                    ((x + shift_x) % ROW_PARTS[0] * ROW_PARTS[1] + (y + shift_y) % ROW_PARTS[1])
                    * ROW_PARTS[2]
                    + (core + shift_core) % ROW_PARTS[2]
                )
                target = (x * ROW_PARTS[1] + y) * ROW_PARTS[2] + core
                pairs.append((source, target))
    return pairs


SHIFTS = ((0, 0), (1, 0), (0, 2), (0, 1), (0, 3), (1, 1), (1, 3), (1, 2))


def joined(blocks):
    half = blocks[0].shape[0] // 2
    return jnp.concatenate([blocks[0][:half], blocks[0][half:], *blocks[1:]], axis=0)


def gather_pieces(own, riders=()):
    def fetch(block, *shift):
        return lax.ppermute(block, "row", row_peers(*shift))

    across = fetch(own, 1, 0, 0)
    opposite, above, below = fetch(own, 0, 2, 0), fetch(own, 0, 1, 0), fetch(own, 0, 3, 0)
    relayed = [fetch(across, 0, 1, 0), fetch(across, 0, 3, 0), fetch(opposite, 1, 0, 0)]
    direct = [own, across, opposite, above, below]
    order = direct + relayed
    early, late = (joined(part) for part in (order[:4], order[4:]))
    early, riders = lax.optimization_barrier((early, riders))
    swapped = [fetch(part, 0, 0, 1) for part in (early, late)]
    return jnp.concatenate(order + swapped, axis=0), riders


def relative_columns(block_columns, blocks_per_device):
    row_id = lax.axis_index("row")
    owner = block_columns // blocks_per_device
    xs, ys, cores = ROW_PARTS
    core = (owner - row_id) % cores
    shift_y = (owner // cores - row_id // cores) % ys
    shift_x = (owner // (cores * ys) - row_id // (cores * ys)) % xs
    piece = sum(
        jnp.where((shift_x == x) & (shift_y == y), index, 0) for index, (x, y) in enumerate(SHIFTS)
    )
    return (core * len(SHIFTS) + piece) * blocks_per_device + block_columns % blocks_per_device


SCALE_ROWS = 8
TOP_EXPONENT = 13.0


def product_kernel(message, keep, columns, values, gathered, *refs):
    count, order, _ = values.shape[1:]
    load_cases = gathered.shape[1]
    earlier, outs = (refs[:0], refs) if message else (refs[:1], refs[1:])

    def one_row(row, largest):
        total = None
        for k in range(count):
            column = pl.multiple_of(columns[row * count + k] * order, order)
            term = jnp.dot(
                values[row, k],
                gathered[pl.ds(column, order), :],
                preferred_element_type=jnp.float32,
            )
            total = term if total is None else total + term
        own_rows = pl.ds(pl.multiple_of(row * order, order), order)
        if keep:
            outs[1][own_rows, :] = total
        if message:
            slice_rows = outs[0].shape[1] - SCALE_ROWS
            parts = order // slice_rows
            for part in range(parts):
                outs[0][row * parts + part, :slice_rows, :] = total[
                    part * slice_rows : (part + 1) * slice_rows, :
                ]
            return jnp.maximum(
                largest, jnp.max(jnp.abs(total).reshape(-1, SCALE_ROWS, load_cases), axis=0)
            )
        outs[0][own_rows, :] = (total - earlier[0][own_rows, :]).astype(outs[0].dtype)
        return largest

    start = jnp.zeros((SCALE_ROWS, load_cases), jnp.float32)
    largest = lax.fori_loop(0, values.shape[0], one_row, start)
    if message:
        top = jnp.full(start.shape, jnp.max(largest), jnp.float32)
        exponent = TOP_EXPONENT - jnp.floor(jnp.log2(jnp.maximum(top, 1e-30)))
        scale = jnp.exp2(exponent)[:1, :]

        def scaled(part, carry):
            slice_rows = outs[0].shape[1] - SCALE_ROWS
            outs[0][part, :slice_rows, :] = outs[0][part, :slice_rows, :] * scale
            outs[0][part, slice_rows:, :] = exponent
            return carry

        lax.fori_loop(0, outs[0].shape[0], scaled, 0)


def block_product(block_values, columns, gathered, slices, earlier=None, keep=False):
    rows, count, order, _ = block_values.shape
    load_cases = gathered.shape[1]
    message = earlier is None
    vmem = pl.BlockSpec(memory_space=pltpu.VMEM)
    whole = (rows * order, load_cases)
    if message:
        outs = [
            jax.ShapeDtypeStruct(
                (slices, rows * order // slices + SCALE_ROWS, load_cases), jnp.float32
            )
        ]
    else:
        outs = [jax.ShapeDtypeStruct(whole, jnp.bfloat16)]
    if keep:
        outs.append(jax.ShapeDtypeStruct(whole, jnp.float32))
    operands = [block_values, gathered] + ([] if message else [earlier])
    return pl.pallas_call(
        functools.partial(product_kernel, message, keep),
        out_shape=outs,
        in_specs=[pl.BlockSpec(memory_space=pltpu.SMEM)] + [vmem] * len(operands),
        out_specs=[vmem] * len(outs),
        compiler_params=pltpu.CompilerParams(vmem_limit_bytes=16 * 1024 * 1024),
        cost_estimate=pl.CostEstimate(
            flops=2 * rows * count * order * order * load_cases,
            bytes_accessed=2 * rows * count * order * order,
            transcendentals=0,
        ),
    )(columns, *operands)


def shifted(cells, distance):
    return [cells[(sector - distance) % len(cells)] for sector in range(len(cells))]


def reduce_coefficients(sub_diag, main_diag, super_diag):
    factors = []
    for exponent in range(LEVELS):
        stride = 2**exponent
        lower = [-a / b for a, b in zip(sub_diag, shifted(main_diag, stride))]
        upper = [-a / b for a, b in zip(super_diag, shifted(main_diag, -stride))]
        factors.append((lower, upper))
        sub_diag, main_diag, super_diag = (
            [a * b for a, b in zip(lower, shifted(sub_diag, stride))],
            [
                main + a * b + c * d
                for main, a, b, c, d in zip(
                    main_diag,
                    lower,
                    shifted(super_diag, stride),
                    upper,
                    shifted(sub_diag, -stride),
                )
            ],
            [a * b for a, b in zip(upper, shifted(super_diag, -stride))],
        )
    return factors, main_diag


def apply_reduction(factors, reduced, right_side):
    for exponent in range(LEVELS):
        stride = 2**exponent
        lower, upper = factors[exponent]
        right_side = [
            own + a * below + b * above
            for own, a, below, b, above in zip(
                right_side,
                lower,
                shifted(right_side, stride),
                upper,
                shifted(right_side, -stride),
            )
        ]
    return [a / b for a, b in zip(right_side, reduced)]


GAINS = 2 * LEVELS
REDUCED, DIAGONAL, COUPLING, KINDS = GAINS + 2, GAINS + 3, GAINS + 4, GAINS + 5


def staging_kernel(cosine_load, sine_load, base, ratio, mistuning, loads, diagonals, couplings, *held):
    *held, arrived = held
    targets = (loads.at[0], loads.at[1], *held)
    copies = [
        pltpu.make_async_copy(source, target, arrived.at[index])
        for index, (source, target) in enumerate(
            zip((cosine_load, sine_load, base, ratio, mistuning), targets)
        )
    ]
    for copy in copies[::-1]:
        copy.start()
    for copy in copies[2:]:
        copy.wait()
    stiffness, spring, deviation = (part[...] for part in held)
    groups, lanes = stiffness.shape
    couplings[...] = spring * stiffness
    for index in range(deviation.shape[0]):
        rows = [
            deviation[index : index + 1, group * lanes : (group + 1) * lanes]
            for group in range(groups)
        ]
        diagonals[index] = stiffness * (1.0 + jnp.concatenate(rows, axis=0))
    for copy in copies[:2]:
        copy.wait()


def coefficient_kernel(classes, own, cosine, sine, diagonals, couplings, loads, rounded, table):
    sectors = table.shape[1]
    coupling = couplings[...]
    diagonal = [diagonals[classes[s]] for s in range(sectors)]
    factors, reduced = reduce_coefficients([-coupling] * sectors, diagonal, [-coupling] * sectors)
    gains = [
        apply_reduction(
            factors, reduced, [jnp.full(coupling.shape, wave[s], jnp.float32) for s in range(sectors)]
        )
        for wave in (cosine, sine)
    ]
    kinds = [part for pair in factors for part in pair]
    kinds += [*gains, reduced, diagonal, [coupling] * sectors]
    for kind, cells in enumerate(kinds):
        for s in range(sectors):
            table[kind, s] = cells[s]
    groups, lanes = coupling.shape
    cosine_gain, sine_gain = table[GAINS, own[0]].T, table[GAINS + 1, own[0]].T
    for group in range(groups):
        rows = pl.ds(group * lanes, lanes)
        rounded[rows, :] = (
            cosine_gain[:, group : group + 1] * loads[0, rows, :]
            + sine_gain[:, group : group + 1] * loads[1, rows, :]
        ).astype(rounded.dtype)


def sector_kernel(last, cosine, sine, table, cosine_load, sine_load, current, *refs):
    products, outs = (refs[:2], refs[2:]) if last else (refs[:1], refs[1:])
    sectors, rows, _ = current.shape
    step = 16
    unscale = [jnp.exp2(-products[0][s, rows : rows + 1, :]) for s in range(sectors)]

    def one_group(group, carry):
        at = pl.ds(pl.multiple_of(group * step, step), step)
        wave_c, wave_s = cosine_load[at, :], sine_load[at, :]
        before = [current[s, at, :] for s in range(sectors)]
        below, above = shifted(before, 1), shifted(before, -1)
        residual = []
        for s in range(sectors):
            forcing = cosine[s] * wave_c + sine[s] * wave_s
            product = products[0][s, at, :] * unscale[s]
            if last:
                product = product + products[1][s, at, :].astype(jnp.float32)
            applied = (
                table[DIAGONAL, s, at, :] * before[s]
                - table[COUPLING, s, at, :] * (below[s] + above[s])
                + product
            )
            residual.append(forcing - applied)
        factors = [
            tuple([table[2 * level + side, s, at, :] for s in range(sectors)] for side in range(2))
            for level in range(LEVELS)
        ]
        reduced = [table[REDUCED, s, at, :] for s in range(sectors)]
        correction = apply_reduction(factors, reduced, residual)
        for s in range(sectors):
            after = before[s] + correction[s]
            if last:
                sent = before[s].astype(jnp.bfloat16).astype(jnp.float32)
                outs[0][s, at, :] = (after - sent).astype(jnp.bfloat16)
            else:
                outs[0][s, at, :] = after.astype(jnp.bfloat16)
                outs[1][s, at, :] = after
        return carry

    lax.fori_loop(0, rows // step, one_group, 0)


def shards(
    cosine_load,
    sine_load,
    base_stiffness,
    coupling_ratio,
    mistuning,
    sector_class,
    engine_order,
    block_values,
    block_columns,
):
    sectors = lax.axis_size("sector")
    sector_id = lax.axis_index("sector")
    local_rows, load_cases = cosine_load.shape
    slice_rows = local_rows // sectors
    smem, vmem = (pl.BlockSpec(memory_space=space) for space in (pltpu.SMEM, pltpu.VMEM))

    def swap(cells):
        return lax.all_to_all(cells, "sector", 0, 0, tiled=True)

    def own_slice(cells, axis):
        return lax.dynamic_slice_in_dim(cells, sector_id * slice_rows, slice_rows, axis)

    all_classes = swap(jnp.broadcast_to(sector_class[:, None], (sectors, 1))).reshape(-1)
    turns = (engine_order[0] * jnp.arange(sectors, dtype=jnp.int32)) % sectors
    angle = turns.astype(jnp.float32) * (2.0 * math.pi / sectors)
    cosine, sine = jnp.cos(angle), jnp.sin(angle)

    lanes = 128
    groups = local_rows // lanes
    loads, diagonals, couplings = pl.pallas_call(
        staging_kernel,
        out_shape=(
            jax.ShapeDtypeStruct((2, local_rows, load_cases), jnp.float32),
            jax.ShapeDtypeStruct((mistuning.shape[0], groups, lanes), jnp.float32),
            jax.ShapeDtypeStruct((groups, lanes), jnp.float32),
        ),
        in_specs=[pl.BlockSpec(memory_space=pl.ANY)] * 5,
        out_specs=(vmem,) * 3,
        scratch_shapes=[
            pltpu.VMEM((groups, lanes), jnp.float32),
            pltpu.VMEM((groups, lanes), jnp.float32),
            pltpu.VMEM(mistuning.shape, jnp.float32),
            pltpu.SemaphoreType.DMA((5,)),
        ],
        compiler_params=pltpu.CompilerParams(vmem_limit_bytes=16 * 1024 * 1024),
    )(
        *[
            pltpu.with_memory_space_constraint(part, pltpu.HBM)
            for part in (
                cosine_load,
                sine_load,
                base_stiffness.reshape(groups, lanes),
                coupling_ratio.reshape(groups, lanes),
                mistuning,
            )
        ]
    )
    rounded, table = pl.pallas_call(
        coefficient_kernel,
        out_shape=(
            jax.ShapeDtypeStruct((local_rows, load_cases), jnp.bfloat16),
            jax.ShapeDtypeStruct((KINDS, sectors, groups, lanes), jnp.float32),
        ),
        in_specs=[smem] * 4 + [vmem] * 3,
        out_specs=(vmem, vmem),
        compiler_params=pltpu.CompilerParams(vmem_limit_bytes=16 * 1024 * 1024),
    )(all_classes, sector_id[None], cosine, sine, diagonals, couplings, loads)
    rounded, loads, block_columns = lax.optimization_barrier((rounded, loads, block_columns))

    cosine_slice, sine_slice = own_slice(loads[0], 0), own_slice(loads[1], 0)
    table = own_slice(table.reshape(KINDS * sectors, local_rows), 1)
    table = jnp.broadcast_to(
        table.reshape(KINDS, sectors, slice_rows, 1), (KINDS, sectors, slice_rows, load_cases)
    )
    current = table[GAINS] * cosine_slice + table[GAINS + 1] * sine_slice

    columns = relative_columns(block_columns, block_values.shape[1]).reshape(-1)
    slice_shape = (sectors, slice_rows, load_cases)
    products = []
    for iteration in range(1, ITERS):
        last = iteration == ITERS - 1
        gathered, (table, current) = gather_pieces(rounded, (table, current))
        if last:
            (change,) = block_product(block_values[0], columns, gathered, sectors, kept)
            products.append(swap(change.reshape(slice_shape)))
        else:
            scaled, *kept = block_product(
                block_values[0], columns, gathered, sectors, keep=iteration == ITERS - 2
            )
            kept = kept[0] if kept else None
            products = [swap(scaled.astype(jnp.float16)).astype(jnp.float32)]
        outs = [jax.ShapeDtypeStruct(slice_shape, jnp.bfloat16)]
        if not last:
            outs.append(jax.ShapeDtypeStruct(slice_shape, jnp.float32))
        outs = pl.pallas_call(
            functools.partial(sector_kernel, last),
            out_shape=outs,
            in_specs=[smem] * 2 + [vmem] * (4 + len(products)),
            out_specs=[vmem] * len(outs),
            compiler_params=pltpu.CompilerParams(vmem_limit_bytes=16 * 1024 * 1024),
        )(cosine, sine, table, cosine_slice, sine_slice, current, *products)
        received = swap(outs[0]).reshape(local_rows, load_cases)
        if last:
            return (rounded.astype(jnp.float32) + received.astype(jnp.float32))[None]
        rounded, current = received, outs[1]


def solution(mesh):
    return jax.shard_map(
        shards,
        mesh=mesh,
        in_specs=(
            P("row", None),
            P("row", None),
            P("row"),
            P("row"),
            P(None, "row"),
            P("sector"),
            P(),
            P("sector", "row", None, None, None),
            P("row", None),
        ),
        out_specs=P("sector", "row", None),
        check_vma=False,
    )
```

```python
import functools
import math

import jax
import jax.numpy as jnp
from jax import lax
from jax.experimental import pallas as pl
from jax.experimental.pallas import tpu as pltpu
from jax.sharding import PartitionSpec as P

ITERS = 4
LEVELS = 3
ROW_PARTS = (2, 4, 2)


def row_peers(shift_x, shift_y, shift_core):
    pairs = []
    for x in range(ROW_PARTS[0]):
        for y in range(ROW_PARTS[1]):
            for core in range(ROW_PARTS[2]):
                source = (
                    ((x + shift_x) % ROW_PARTS[0] * ROW_PARTS[1] + (y + shift_y) % ROW_PARTS[1])
                    * ROW_PARTS[2]
                    + (core + shift_core) % ROW_PARTS[2]
                )
                target = (x * ROW_PARTS[1] + y) * ROW_PARTS[2] + core
                pairs.append((source, target))
    return pairs


SHIFTS = ((0, 0), (1, 0), (0, 2), (0, 1), (0, 3), (1, 1), (1, 3), (1, 2))


def joined(blocks):
    half = blocks[0].shape[0] // 2
    return jnp.concatenate([blocks[0][:half], blocks[0][half:], *blocks[1:]], axis=0)


def gather_pieces(own, riders=()):
    def fetch(block, *shift):
        return lax.ppermute(block, "row", row_peers(*shift))

    opposite, across = fetch(own, 0, 2, 0), fetch(own, 1, 0, 0)
    above, below = fetch(own, 0, 1, 0), fetch(own, 0, 3, 0)
    opposite, across = lax.optimization_barrier((opposite, across))
    relayed = [fetch(across, 0, 1, 0), fetch(across, 0, 3, 0), fetch(opposite, 1, 0, 0)]
    direct = [own, across, opposite, above, below]
    order = direct + relayed
    early, late = (joined(part) for part in (order[:4], order[4:]))
    early, riders = lax.optimization_barrier((early, riders))
    swapped = [fetch(part, 0, 0, 1) for part in (early, late)]
    return jnp.concatenate(order + swapped, axis=0), riders


def relative_columns(block_columns, blocks_per_device):
    row_id = lax.axis_index("row")
    owner = block_columns // blocks_per_device
    xs, ys, cores = ROW_PARTS
    core = (owner - row_id) % cores
    shift_y = (owner // cores - row_id // cores) % ys
    shift_x = (owner // (cores * ys) - row_id // (cores * ys)) % xs
    piece = sum(
        jnp.where((shift_x == x) & (shift_y == y), index, 0) for index, (x, y) in enumerate(SHIFTS)
    )
    return (core * len(SHIFTS) + piece) * blocks_per_device + block_columns % blocks_per_device


SCALE_ROWS = 8
TOP_EXPONENT = 13.0


def product_kernel(message, keep, columns, values, gathered, *refs):
    count, order, _ = values.shape[1:]
    load_cases = gathered.shape[1]
    earlier, outs = (refs[:0], refs) if message else (refs[:1], refs[1:])

    def one_row(row, largest):
        total = None
        for k in range(count):
            column = pl.multiple_of(columns[row * count + k] * order, order)
            term = jnp.dot(
                values[row, k],
                gathered[pl.ds(column, order), :],
                preferred_element_type=jnp.float32,
            )
            total = term if total is None else total + term
        own_rows = pl.ds(pl.multiple_of(row * order, order), order)
        if keep:
            outs[1][own_rows, :] = total
        if message:
            slice_rows = outs[0].shape[1] - SCALE_ROWS
            parts = order // slice_rows
            for part in range(parts):
                outs[0][row * parts + part, :slice_rows, :] = total[
                    part * slice_rows : (part + 1) * slice_rows, :
                ]
            return jnp.maximum(
                largest, jnp.max(jnp.abs(total).reshape(-1, SCALE_ROWS, load_cases), axis=0)
            )
        outs[0][own_rows, :] = (total - earlier[0][own_rows, :]).astype(outs[0].dtype)
        return largest

    start = jnp.zeros((SCALE_ROWS, load_cases), jnp.float32)
    largest = lax.fori_loop(0, values.shape[0], one_row, start)
    if message:
        top = jnp.full(start.shape, jnp.max(largest), jnp.float32)
        exponent = TOP_EXPONENT - jnp.floor(jnp.log2(jnp.maximum(top, 1e-30)))
        scale = jnp.exp2(exponent)[:1, :]

        def scaled(part, carry):
            slice_rows = outs[0].shape[1] - SCALE_ROWS
            outs[0][part, :slice_rows, :] = outs[0][part, :slice_rows, :] * scale
            outs[0][part, slice_rows:, :] = exponent
            return carry

        lax.fori_loop(0, outs[0].shape[0], scaled, 0)


def block_product(block_values, columns, gathered, slices, earlier=None, keep=False):
    rows, count, order, _ = block_values.shape
    load_cases = gathered.shape[1]
    message = earlier is None
    vmem = pl.BlockSpec(memory_space=pltpu.VMEM)
    whole = (rows * order, load_cases)
    if message:
        outs = [
            jax.ShapeDtypeStruct(
                (slices, rows * order // slices + SCALE_ROWS, load_cases), jnp.float32
            )
        ]
    else:
        outs = [jax.ShapeDtypeStruct(whole, jnp.bfloat16)]
    if keep:
        outs.append(jax.ShapeDtypeStruct(whole, jnp.float32))
    operands = [block_values, gathered] + ([] if message else [earlier])
    return pl.pallas_call(
        functools.partial(product_kernel, message, keep),
        out_shape=outs,
        in_specs=[pl.BlockSpec(memory_space=pltpu.SMEM)] + [vmem] * len(operands),
        out_specs=[vmem] * len(outs),
        compiler_params=pltpu.CompilerParams(vmem_limit_bytes=16 * 1024 * 1024),
        cost_estimate=pl.CostEstimate(
            flops=2 * rows * count * order * order * load_cases,
            bytes_accessed=2 * rows * count * order * order,
            transcendentals=0,
        ),
    )(columns, *operands)


def shifted(cells, distance):
    return [cells[(sector - distance) % len(cells)] for sector in range(len(cells))]


def reduce_coefficients(sub_diag, main_diag, super_diag):
    factors = []
    for exponent in range(LEVELS):
        stride = 2**exponent
        lower = [-a / b for a, b in zip(sub_diag, shifted(main_diag, stride))]
        upper = [-a / b for a, b in zip(super_diag, shifted(main_diag, -stride))]
        factors.append((lower, upper))
        sub_diag, main_diag, super_diag = (
            [a * b for a, b in zip(lower, shifted(sub_diag, stride))],
            [
                main + a * b + c * d
                for main, a, b, c, d in zip(
                    main_diag,
                    lower,
                    shifted(super_diag, stride),
                    upper,
                    shifted(sub_diag, -stride),
                )
            ],
            [a * b for a, b in zip(upper, shifted(super_diag, -stride))],
        )
    return factors, main_diag


def apply_reduction(factors, reduced, right_side):
    for exponent in range(LEVELS):
        stride = 2**exponent
        lower, upper = factors[exponent]
        right_side = [
            own + a * below + b * above
            for own, a, below, b, above in zip(
                right_side,
                lower,
                shifted(right_side, stride),
                upper,
                shifted(right_side, -stride),
            )
        ]
    return [a / b for a, b in zip(right_side, reduced)]


GAINS = 2 * LEVELS
REDUCED, DIAGONAL, COUPLING, KINDS = GAINS + 2, GAINS + 3, GAINS + 4, GAINS + 5


def staging_kernel(cosine_load, sine_load, base, ratio, mistuning, loads, diagonals, couplings, *held):
    *held, arrived = held
    targets = (loads.at[0], loads.at[1], *held)
    copies = [
        pltpu.make_async_copy(source, target, arrived.at[index])
        for index, (source, target) in enumerate(
            zip((cosine_load, sine_load, base, ratio, mistuning), targets)
        )
    ]
    for copy in copies[::-1]:
        copy.start()
    for copy in copies[2:]:
        copy.wait()
    stiffness, spring, deviation = (part[...] for part in held)
    groups, lanes = stiffness.shape
    couplings[...] = spring * stiffness
    for index in range(deviation.shape[0]):
        rows = [
            deviation[index : index + 1, group * lanes : (group + 1) * lanes]
            for group in range(groups)
        ]
        diagonals[index] = stiffness * (1.0 + jnp.concatenate(rows, axis=0))
    for copy in copies[:2]:
        copy.wait()


def coefficient_kernel(classes, own, cosine, sine, diagonals, couplings, loads, rounded, table):
    sectors = table.shape[1]
    coupling = couplings[...]
    diagonal = [diagonals[classes[s]] for s in range(sectors)]
    factors, reduced = reduce_coefficients([-coupling] * sectors, diagonal, [-coupling] * sectors)
    gains = [
        apply_reduction(
            factors, reduced, [jnp.full(coupling.shape, wave[s], jnp.float32) for s in range(sectors)]
        )
        for wave in (cosine, sine)
    ]
    kinds = [part for pair in factors for part in pair]
    kinds += [*gains, reduced, diagonal, [coupling] * sectors]
    for kind, cells in enumerate(kinds):
        for s in range(sectors):
            table[kind, s] = cells[s]
    groups, lanes = coupling.shape
    cosine_gain, sine_gain = table[GAINS, own[0]].T, table[GAINS + 1, own[0]].T
    for group in range(groups):
        rows = pl.ds(group * lanes, lanes)
        rounded[rows, :] = (
            cosine_gain[:, group : group + 1] * loads[0, rows, :]
            + sine_gain[:, group : group + 1] * loads[1, rows, :]
        ).astype(rounded.dtype)


def sector_kernel(last, cosine, sine, table, cosine_load, sine_load, current, *refs):
    products, outs = (refs[:2], refs[2:]) if last else (refs[:1], refs[1:])
    sectors, rows, _ = current.shape
    step = 16
    unscale = [jnp.exp2(-products[0][s, rows : rows + 1, :]) for s in range(sectors)]

    def one_group(group, carry):
        at = pl.ds(pl.multiple_of(group * step, step), step)
        wave_c, wave_s = cosine_load[at, :], sine_load[at, :]
        before = [current[s, at, :] for s in range(sectors)]
        below, above = shifted(before, 1), shifted(before, -1)
        residual = []
        for s in range(sectors):
            forcing = cosine[s] * wave_c + sine[s] * wave_s
            product = products[0][s, at, :] * unscale[s]
            if last:
                product = product + products[1][s, at, :].astype(jnp.float32)
            applied = (
                table[DIAGONAL, s, at, :] * before[s]
                - table[COUPLING, s, at, :] * (below[s] + above[s])
                + product
            )
            residual.append(forcing - applied)
        factors = [
            tuple([table[2 * level + side, s, at, :] for s in range(sectors)] for side in range(2))
            for level in range(LEVELS)
        ]
        reduced = [table[REDUCED, s, at, :] for s in range(sectors)]
        correction = apply_reduction(factors, reduced, residual)
        for s in range(sectors):
            after = before[s] + correction[s]
            if last:
                sent = before[s].astype(jnp.bfloat16).astype(jnp.float32)
                outs[0][s, at, :] = (after - sent).astype(jnp.bfloat16)
            else:
                outs[0][s, at, :] = after.astype(jnp.bfloat16)
                outs[1][s, at, :] = after
        return carry

    lax.fori_loop(0, rows // step, one_group, 0)


def shards(
    cosine_load,
    sine_load,
    base_stiffness,
    coupling_ratio,
    mistuning,
    sector_class,
    engine_order,
    block_values,
    block_columns,
):
    sectors = lax.axis_size("sector")
    sector_id = lax.axis_index("sector")
    local_rows, load_cases = cosine_load.shape
    slice_rows = local_rows // sectors
    smem, vmem = (pl.BlockSpec(memory_space=space) for space in (pltpu.SMEM, pltpu.VMEM))

    def swap(cells):
        return lax.all_to_all(cells, "sector", 0, 0, tiled=True)

    def own_slice(cells, axis):
        return lax.dynamic_slice_in_dim(cells, sector_id * slice_rows, slice_rows, axis)

    all_classes = swap(jnp.broadcast_to(sector_class[:, None], (sectors, 1))).reshape(-1)
    turns = (engine_order[0] * jnp.arange(sectors, dtype=jnp.int32)) % sectors
    angle = turns.astype(jnp.float32) * (2.0 * math.pi / sectors)
    cosine, sine = jnp.cos(angle), jnp.sin(angle)

    lanes = 128
    groups = local_rows // lanes
    loads, diagonals, couplings = pl.pallas_call(
        staging_kernel,
        out_shape=(
            jax.ShapeDtypeStruct((2, local_rows, load_cases), jnp.float32),
            jax.ShapeDtypeStruct((mistuning.shape[0], groups, lanes), jnp.float32),
            jax.ShapeDtypeStruct((groups, lanes), jnp.float32),
        ),
        in_specs=[pl.BlockSpec(memory_space=pl.ANY)] * 5,
        out_specs=(vmem,) * 3,
        scratch_shapes=[
            pltpu.VMEM((groups, lanes), jnp.float32),
            pltpu.VMEM((groups, lanes), jnp.float32),
            pltpu.VMEM(mistuning.shape, jnp.float32),
            pltpu.SemaphoreType.DMA((5,)),
        ],
        compiler_params=pltpu.CompilerParams(vmem_limit_bytes=16 * 1024 * 1024),
    )(
        *[
            pltpu.with_memory_space_constraint(part, pltpu.HBM)
            for part in (
                cosine_load,
                sine_load,
                base_stiffness.reshape(groups, lanes),
                coupling_ratio.reshape(groups, lanes),
                mistuning,
            )
        ]
    )
    rounded, table = pl.pallas_call(
        coefficient_kernel,
        out_shape=(
            jax.ShapeDtypeStruct((local_rows, load_cases), jnp.bfloat16),
            jax.ShapeDtypeStruct((KINDS, sectors, groups, lanes), jnp.float32),
        ),
        in_specs=[smem] * 4 + [vmem] * 3,
        out_specs=(vmem, vmem),
        compiler_params=pltpu.CompilerParams(vmem_limit_bytes=16 * 1024 * 1024),
    )(all_classes, sector_id[None], cosine, sine, diagonals, couplings, loads)
    rounded, loads, block_columns = lax.optimization_barrier((rounded, loads, block_columns))

    cosine_slice, sine_slice = own_slice(loads[0], 0), own_slice(loads[1], 0)
    table = own_slice(table.reshape(KINDS * sectors, local_rows), 1)
    table = jnp.broadcast_to(
        table.reshape(KINDS, sectors, slice_rows, 1), (KINDS, sectors, slice_rows, load_cases)
    )
    current = table[GAINS] * cosine_slice + table[GAINS + 1] * sine_slice

    columns = relative_columns(block_columns, block_values.shape[1]).reshape(-1)
    slice_shape = (sectors, slice_rows, load_cases)
    products = []
    for iteration in range(1, ITERS):
        last = iteration == ITERS - 1
        gathered, (table, current) = gather_pieces(rounded, (table, current))
        if last:
            (change,) = block_product(block_values[0], columns, gathered, sectors, kept)
            products.append(swap(change.reshape(slice_shape)))
        else:
            scaled, *kept = block_product(
                block_values[0], columns, gathered, sectors, keep=iteration == ITERS - 2
            )
            kept = kept[0] if kept else None
            products = [swap(scaled.astype(jnp.float16)).astype(jnp.float32)]
        outs = [jax.ShapeDtypeStruct(slice_shape, jnp.bfloat16)]
        if not last:
            outs.append(jax.ShapeDtypeStruct(slice_shape, jnp.float32))
        outs = pl.pallas_call(
            functools.partial(sector_kernel, last),
            out_shape=outs,
            in_specs=[smem] * 2 + [vmem] * (4 + len(products)),
            out_specs=[vmem] * len(outs),
            compiler_params=pltpu.CompilerParams(vmem_limit_bytes=16 * 1024 * 1024),
        )(cosine, sine, table, cosine_slice, sine_slice, current, *products)
        received = swap(outs[0]).reshape(local_rows, load_cases)
        if last:
            return (rounded.astype(jnp.float32) + received.astype(jnp.float32))[None]
        rounded, current = received, outs[1]


def solution(mesh):
    return jax.shard_map(
        shards,
        mesh=mesh,
        in_specs=(
            P("row", None),
            P("row", None),
            P("row"),
            P("row"),
            P(None, "row"),
            P("sector"),
            P(),
            P("sector", "row", None, None, None),
            P("row", None),
        ),
        out_specs=P("sector", "row", None),
        check_vma=False,
    )
```

```python
import functools
import math

import jax
import jax.numpy as jnp
from jax import lax
from jax.experimental import pallas as pl
from jax.experimental.pallas import tpu as pltpu
from jax.sharding import PartitionSpec as P

ITERS = 4
LEVELS = 3
ROW_PARTS = (2, 4, 2)


def row_peers(shift_x, shift_y, shift_core):
    pairs = []
    for x in range(ROW_PARTS[0]):
        for y in range(ROW_PARTS[1]):
            for core in range(ROW_PARTS[2]):
                source = (
                    ((x + shift_x) % ROW_PARTS[0] * ROW_PARTS[1] + (y + shift_y) % ROW_PARTS[1])
                    * ROW_PARTS[2]
                    + (core + shift_core) % ROW_PARTS[2]
                )
                target = (x * ROW_PARTS[1] + y) * ROW_PARTS[2] + core
                pairs.append((source, target))
    return pairs


SHIFTS = ((0, 0), (1, 0), (0, 2), (0, 1), (0, 3), (1, 1), (1, 3), (1, 2))


def joined(blocks):
    half = blocks[0].shape[0] // 2
    return jnp.concatenate([blocks[0][:half], blocks[0][half:], *blocks[1:]], axis=0)


def gather_pieces(own, riders=()):
    def fetch(block, *shift):
        return lax.ppermute(block, "row", row_peers(*shift))

    across = fetch(own, 1, 0, 0)
    opposite, above, below = fetch(own, 0, 2, 0), fetch(own, 0, 1, 0), fetch(own, 0, 3, 0)
    relayed = [fetch(across, 0, 1, 0), fetch(across, 0, 3, 0), fetch(opposite, 1, 0, 0)]
    direct = [own, across, opposite, above, below]
    order = direct + relayed
    early, late = (joined(part) for part in (order[:4], order[4:]))
    early, riders = lax.optimization_barrier((early, riders))
    swapped = [fetch(part, 0, 0, 1) for part in (early, late)]
    return jnp.concatenate(order + swapped, axis=0), riders


def relative_columns(block_columns, blocks_per_device):
    row_id = lax.axis_index("row")
    owner = block_columns // blocks_per_device
    xs, ys, cores = ROW_PARTS
    core = (owner - row_id) % cores
    shift_y = (owner // cores - row_id // cores) % ys
    shift_x = (owner // (cores * ys) - row_id // (cores * ys)) % xs
    piece = sum(
        jnp.where((shift_x == x) & (shift_y == y), index, 0) for index, (x, y) in enumerate(SHIFTS)
    )
    return (core * len(SHIFTS) + piece) * blocks_per_device + block_columns % blocks_per_device


SCALE_ROWS = 8
TOP_EXPONENT = 13.0


def product_kernel(message, keep, columns, values, gathered, *refs):
    count, order, _ = values.shape[1:]
    load_cases = gathered.shape[1]
    earlier, outs = (refs[:0], refs) if message else (refs[:1], refs[1:])

    def one_row(row, largest):
        total = None
        for k in range(count):
            column = pl.multiple_of(columns[row * count + k] * order, order)
            term = jnp.dot(
                values[row, k],
                gathered[pl.ds(column, order), :],
                preferred_element_type=jnp.float32,
            )
            total = term if total is None else total + term
        own_rows = pl.ds(pl.multiple_of(row * order, order), order)
        if keep:
            outs[1][own_rows, :] = total
        if message:
            slice_rows = outs[0].shape[1] - SCALE_ROWS
            parts = order // slice_rows
            for part in range(parts):
                outs[0][row * parts + part, :slice_rows, :] = total[
                    part * slice_rows : (part + 1) * slice_rows, :
                ]
            return jnp.maximum(
                largest, jnp.max(jnp.abs(total).reshape(-1, SCALE_ROWS, load_cases), axis=0)
            )
        outs[0][own_rows, :] = (total - earlier[0][own_rows, :]).astype(outs[0].dtype)
        return largest

    start = jnp.zeros((SCALE_ROWS, load_cases), jnp.float32)
    largest = lax.fori_loop(0, values.shape[0], one_row, start)
    if message:
        top = jnp.full(start.shape, jnp.max(largest), jnp.float32)
        exponent = TOP_EXPONENT - jnp.floor(jnp.log2(jnp.maximum(top, 1e-30)))
        scale = jnp.exp2(exponent)[:1, :]

        def scaled(part, carry):
            slice_rows = outs[0].shape[1] - SCALE_ROWS
            outs[0][part, :slice_rows, :] = outs[0][part, :slice_rows, :] * scale
            outs[0][part, slice_rows:, :] = exponent
            return carry

        lax.fori_loop(0, outs[0].shape[0], scaled, 0)


def block_product(block_values, columns, gathered, slices, earlier=None, keep=False):
    rows, count, order, _ = block_values.shape
    load_cases = gathered.shape[1]
    message = earlier is None
    vmem = pl.BlockSpec(memory_space=pltpu.VMEM)
    whole = (rows * order, load_cases)
    if message:
        outs = [
            jax.ShapeDtypeStruct(
                (slices, rows * order // slices + SCALE_ROWS, load_cases), jnp.float32
            )
        ]
    else:
        outs = [jax.ShapeDtypeStruct(whole, jnp.bfloat16)]
    if keep:
        outs.append(jax.ShapeDtypeStruct(whole, jnp.float32))
    operands = [block_values, gathered] + ([] if message else [earlier])
    return pl.pallas_call(
        functools.partial(product_kernel, message, keep),
        out_shape=outs,
        in_specs=[pl.BlockSpec(memory_space=pltpu.SMEM)] + [vmem] * len(operands),
        out_specs=[vmem] * len(outs),
        compiler_params=pltpu.CompilerParams(vmem_limit_bytes=16 * 1024 * 1024),
        cost_estimate=pl.CostEstimate(
            flops=2 * rows * count * order * order * load_cases,
            bytes_accessed=2 * rows * count * order * order,
            transcendentals=0,
        ),
    )(columns, *operands)


def shifted(cells, distance):
    return [cells[(sector - distance) % len(cells)] for sector in range(len(cells))]


def reduce_coefficients(sub_diag, main_diag, super_diag):
    factors = []
    for exponent in range(LEVELS):
        stride = 2**exponent
        lower = [-a / b for a, b in zip(sub_diag, shifted(main_diag, stride))]
        upper = [-a / b for a, b in zip(super_diag, shifted(main_diag, -stride))]
        factors.append((lower, upper))
        sub_diag, main_diag, super_diag = (
            [a * b for a, b in zip(lower, shifted(sub_diag, stride))],
            [
                main + a * b + c * d
                for main, a, b, c, d in zip(
                    main_diag,
                    lower,
                    shifted(super_diag, stride),
                    upper,
                    shifted(sub_diag, -stride),
                )
            ],
            [a * b for a, b in zip(upper, shifted(super_diag, -stride))],
        )
    return factors, main_diag


def apply_reduction(factors, reduced, right_side):
    for exponent in range(LEVELS):
        stride = 2**exponent
        lower, upper = factors[exponent]
        right_side = [
            own + a * below + b * above
            for own, a, below, b, above in zip(
                right_side,
                lower,
                shifted(right_side, stride),
                upper,
                shifted(right_side, -stride),
            )
        ]
    return [a / b for a, b in zip(right_side, reduced)]


GAINS = 2 * LEVELS
REDUCED, DIAGONAL, COUPLING, KINDS = GAINS + 2, GAINS + 3, GAINS + 4, GAINS + 5


def staging_kernel(cosine_load, sine_load, base, ratio, mistuning, loads, diagonals, couplings, *held):
    *held, arrived = held
    targets = (loads.at[0], loads.at[1], *held)
    copies = [
        pltpu.make_async_copy(source, target, arrived.at[index])
        for index, (source, target) in enumerate(
            zip((cosine_load, sine_load, base, ratio, mistuning), targets)
        )
    ]
    for copy in copies[::-1]:
        copy.start()
    for copy in copies[2:]:
        copy.wait()
    stiffness, spring, deviation = (part[...] for part in held)
    groups, lanes = stiffness.shape
    couplings[...] = spring * stiffness
    for index in range(deviation.shape[0]):
        rows = [
            deviation[index : index + 1, group * lanes : (group + 1) * lanes]
            for group in range(groups)
        ]
        diagonals[index] = stiffness * (1.0 + jnp.concatenate(rows, axis=0))
    for copy in copies[:2]:
        copy.wait()


def coefficient_kernel(classes, own, cosine, sine, diagonals, couplings, loads, rounded, table):
    sectors = table.shape[1]
    coupling = couplings[...]
    diagonal = [diagonals[classes[s, 0]] for s in range(sectors)]
    factors, reduced = reduce_coefficients([-coupling] * sectors, diagonal, [-coupling] * sectors)
    gains = [
        apply_reduction(
            factors, reduced, [jnp.full(coupling.shape, wave[s], jnp.float32) for s in range(sectors)]
        )
        for wave in (cosine, sine)
    ]
    kinds = [part for pair in factors for part in pair]
    kinds += [*gains, reduced, diagonal, [coupling] * sectors]
    for kind, cells in enumerate(kinds):
        for s in range(sectors):
            table[kind, s] = cells[s]
    groups, lanes = coupling.shape
    cosine_gain, sine_gain = table[GAINS, own[0]].T, table[GAINS + 1, own[0]].T
    for group in range(groups):
        rows = pl.ds(group * lanes, lanes)
        rounded[rows, :] = (
            cosine_gain[:, group : group + 1] * loads[0, rows, :]
            + sine_gain[:, group : group + 1] * loads[1, rows, :]
        ).astype(rounded.dtype)


def sector_kernel(last, cosine, sine, table, cosine_load, sine_load, current, *refs):
    products, outs = (refs[:2], refs[2:]) if last else (refs[:1], refs[1:])
    sectors, rows, _ = current.shape
    step = 16
    unscale = [jnp.exp2(-products[0][s, rows : rows + 1, :]) for s in range(sectors)]

    def one_group(group, carry):
        at = pl.ds(pl.multiple_of(group * step, step), step)
        wave_c, wave_s = cosine_load[at, :], sine_load[at, :]
        before = [current[s, at, :] for s in range(sectors)]
        below, above = shifted(before, 1), shifted(before, -1)
        residual = []
        for s in range(sectors):
            forcing = cosine[s] * wave_c + sine[s] * wave_s
            product = products[0][s, at, :] * unscale[s]
            if last:
                product = product + products[1][s, at, :].astype(jnp.float32)
            applied = (
                table[DIAGONAL, s, at, :] * before[s]
                - table[COUPLING, s, at, :] * (below[s] + above[s])
                + product
            )
            residual.append(forcing - applied)
        factors = [
            tuple([table[2 * level + side, s, at, :] for s in range(sectors)] for side in range(2))
            for level in range(LEVELS)
        ]
        reduced = [table[REDUCED, s, at, :] for s in range(sectors)]
        correction = apply_reduction(factors, reduced, residual)
        for s in range(sectors):
            after = before[s] + correction[s]
            if last:
                sent = before[s].astype(jnp.bfloat16).astype(jnp.float32)
                outs[0][s, at, :] = (after - sent).astype(jnp.bfloat16)
            else:
                outs[0][s, at, :] = after.astype(jnp.bfloat16)
                outs[1][s, at, :] = after
        return carry

    lax.fori_loop(0, rows // step, one_group, 0)


def shards(
    cosine_load,
    sine_load,
    base_stiffness,
    coupling_ratio,
    mistuning,
    sector_class,
    engine_order,
    block_values,
    block_columns,
):
    sectors = lax.axis_size("sector")
    sector_id = lax.axis_index("sector")
    local_rows, load_cases = cosine_load.shape
    slice_rows = local_rows // sectors
    smem, vmem = (pl.BlockSpec(memory_space=space) for space in (pltpu.SMEM, pltpu.VMEM))

    def swap(cells):
        return lax.all_to_all(cells, "sector", 0, 0, tiled=True)

    def own_slice(cells, axis):
        return lax.dynamic_slice_in_dim(cells, sector_id * slice_rows, slice_rows, axis)

    all_classes = swap(jnp.broadcast_to(sector_class[:, None], (sectors, 1)))
    turns = (engine_order[0] * jnp.arange(sectors, dtype=jnp.int32)) % sectors
    angle = turns.astype(jnp.float32) * (2.0 * math.pi / sectors)
    cosine, sine = jnp.cos(angle), jnp.sin(angle)

    lanes = 128
    groups = local_rows // lanes
    loads, diagonals, couplings = pl.pallas_call(
        staging_kernel,
        out_shape=(
            jax.ShapeDtypeStruct((2, local_rows, load_cases), jnp.float32),
            jax.ShapeDtypeStruct((mistuning.shape[0], groups, lanes), jnp.float32),
            jax.ShapeDtypeStruct((groups, lanes), jnp.float32),
        ),
        in_specs=[pl.BlockSpec(memory_space=pl.ANY)] * 5,
        out_specs=(vmem,) * 3,
        scratch_shapes=[
            pltpu.VMEM((groups, lanes), jnp.float32),
            pltpu.VMEM((groups, lanes), jnp.float32),
            pltpu.VMEM(mistuning.shape, jnp.float32),
            pltpu.SemaphoreType.DMA((5,)),
        ],
        compiler_params=pltpu.CompilerParams(vmem_limit_bytes=16 * 1024 * 1024),
    )(
        *[
            pltpu.with_memory_space_constraint(part, pltpu.HBM)
            for part in (
                cosine_load,
                sine_load,
                base_stiffness.reshape(groups, lanes),
                coupling_ratio.reshape(groups, lanes),
                mistuning,
            )
        ]
    )
    rounded, table = pl.pallas_call(
        coefficient_kernel,
        out_shape=(
            jax.ShapeDtypeStruct((local_rows, load_cases), jnp.bfloat16),
            jax.ShapeDtypeStruct((KINDS, sectors, groups, lanes), jnp.float32),
        ),
        in_specs=[smem] * 4 + [vmem] * 3,
        out_specs=(vmem, vmem),
        compiler_params=pltpu.CompilerParams(vmem_limit_bytes=16 * 1024 * 1024),
    )(all_classes, sector_id[None], cosine, sine, diagonals, couplings, loads)
    rounded, loads, block_columns = lax.optimization_barrier((rounded, loads, block_columns))

    cosine_slice, sine_slice = own_slice(loads[0], 0), own_slice(loads[1], 0)
    table = own_slice(table.reshape(KINDS * sectors, local_rows), 1)
    table = jnp.broadcast_to(
        table.reshape(KINDS, sectors, slice_rows, 1), (KINDS, sectors, slice_rows, load_cases)
    )
    current = table[GAINS] * cosine_slice + table[GAINS + 1] * sine_slice

    columns = relative_columns(block_columns, block_values.shape[1]).reshape(-1)
    slice_shape = (sectors, slice_rows, load_cases)
    products = []
    for iteration in range(1, ITERS):
        last = iteration == ITERS - 1
        gathered, (table, current) = gather_pieces(rounded, (table, current))
        if last:
            (change,) = block_product(block_values[0], columns, gathered, sectors, kept)
            products.append(swap(change.reshape(slice_shape)))
        else:
            scaled, *kept = block_product(
                block_values[0], columns, gathered, sectors, keep=iteration == ITERS - 2
            )
            kept = kept[0] if kept else None
            products = [swap(scaled.astype(jnp.float16)).astype(jnp.float32)]
        outs = [jax.ShapeDtypeStruct(slice_shape, jnp.bfloat16)]
        if not last:
            outs.append(jax.ShapeDtypeStruct(slice_shape, jnp.float32))
        outs = pl.pallas_call(
            functools.partial(sector_kernel, last),
            out_shape=outs,
            in_specs=[smem] * 2 + [vmem] * (4 + len(products)),
            out_specs=[vmem] * len(outs),
            compiler_params=pltpu.CompilerParams(vmem_limit_bytes=16 * 1024 * 1024),
        )(cosine, sine, table, cosine_slice, sine_slice, current, *products)
        received = swap(outs[0]).reshape(local_rows, load_cases)
        if last:
            return (rounded.astype(jnp.float32) + received.astype(jnp.float32))[None]
        rounded, current = received, outs[1]


def solution(mesh):
    return jax.shard_map(
        shards,
        mesh=mesh,
        in_specs=(
            P("row", None),
            P("row", None),
            P("row"),
            P("row"),
            P(None, "row"),
            P("sector"),
            P(),
            P("sector", "row", None, None, None),
            P("row", None),
        ),
        out_specs=P("sector", "row", None),
        check_vma=False,
    )
```
